512 devices in a mesh: ctx: 32 (over z, x), tp: 16 (over y, core).
Axes of the slice: x: 4, y: 8, z: 8, core: 2. Of those that a mesh axis runs over, the one named last changes fastest.
Arguments:
- features: bfloat16 [16384, 3, 4096], P(('ctx', 'tp')), may hold values from -6 to 6
- residual: bfloat16 [16384, 4096], P(('ctx', 'tp')), may hold values from -6 to 6
- short_weight: float32 [7, 3, 4096], P(None, None, 'tp'), may hold values from -2 to 2
- rates: float32 [256, 16], P('tp'), may hold values from 3.0517578e-05 to 0.06
- residues: float32 [256, 16], P('tp'), may hold values from -1.5 to 1.5
- out_weight: bfloat16 [4096, 4096], P('tp'), may hold values from -0.09375 to 0.09375
Outputs:
- mixed: bfloat16 [16384, 4096], P(('ctx', 'tp'))
The draws below stay inside these ranges and needn't reach their ends.
All inputs are finite; a program needn't handle non-finite values.
Results may differ from the reference program's by a relative error of at most 0.023.
Values may be sent and summed in bfloat16 or wider, within the bound.
A program may use at most 64 MiB of HBM per device.

```python
import math
import jax
import jax.numpy as jnp
from jax import lax

D = 4096
ORDER = 16
GROUP_CH = 16
TOK_CTX = 512
TOKENS = 16384
GROUPS = 256
N_CTX = 32
N_TP = 16


def block_scale(key, dims, split, least, high):
    def one(dim, shards_of):
        steps = jax.random.uniform(jax.random.fold_in(jax.random.fold_in(key, 6), dim), (shards_of,), jnp.float32, least / len(split), high / len(split))
        return jnp.repeat(jnp.exp(steps), dims[dim] // shards_of).reshape((-1,) + (1,) * (len(dims) - dim - 1))

    loudness = one(*split[0])
    for cut in split[1:]:
        loudness = loudness * one(*cut)
    return loudness


def centred(own_key, dims, scale, limit, cuts=(), kind=jnp.bfloat16):
    values = jax.random.normal(own_key, dims, jnp.float32) * scale
    if len(cuts) > 0:
        values = block_scale(own_key, dims, cuts, -0.22, 0.18) * values
    return jnp.clip(values, min=-limit, max=limit).astype(kind)


def setup_inputs(seed: int = 0) -> dict:
    key_list = jax.random.split(jax.random.key(seed), 7)
    features = centred(key_list[0], (TOKENS, 3, D), 1.0, 6.0, ((0, 512),))
    residual = centred(key_list[1], (TOKENS, D), 1.0, 6.0, ((0, 512),))
    short_weight = centred(key_list[2], (7, 3, D), 7 ** -0.5, 2.0, ((2, 16),), jnp.float32)
    rates = jnp.clip(jnp.exp(math.log(0.06) - 7.583797 * jax.random.uniform(key_list[3], (GROUPS, ORDER), jnp.float32) ** block_scale(key_list[3], (GROUPS, ORDER), ((0, 16),), -0.2, 0.2)), 3.0517578125e-05, 0.06)
    residues = centred(key_list[4], (GROUPS, ORDER), 0.25, 1.5, ((0, 16),), jnp.float32)
    out_weight = centred(key_list[5], (D, D), D ** -0.5, 0.09375, ((0, 16),))
    return {"features": features, "residual": residual, "short_weight": short_weight, "rates": rates, "residues": residues, "out_weight": out_weight}


precise_mode = lax.Precision.HIGHEST

def local_terms(product, rates, coefs):
    block_len = product.shape[0]
    steps_idx = jnp.arange(block_len, dtype=jnp.int32)
    valid = steps_idx[:, None] >= steps_idx[None, :]
    position = steps_idx.astype(jnp.float32)
    falling = coefs[:, :, None] * jnp.exp(-rates[:, :, None] * position)
    rising = jnp.exp(rates[:, :, None] * position)
    matrix = jnp.einsum('gnt,gns->gts', falling, rising, precision=precise_mode)
    matrix = jnp.where(valid[None], matrix, 0.0)
    local = jnp.einsum('gts,sgc->gtc', matrix, product, precision=precise_mode)
    outof = jnp.exp(-rates[:, :, None] * (block_len - 1.0 - position))
    state_here = jnp.einsum('gnt,tgc->ngc', outof, product, precision=precise_mode)
    return (local, state_here)

def carry_terms(rates, coefs, state_in, block_len):
    position = jnp.arange(block_len, dtype=jnp.int32).astype(jnp.float32)
    into = coefs[:, :, None] * jnp.exp(-rates[:, :, None] * (position + 1.0))
    return jnp.einsum('gnt,ngc->gtc', into, state_in, precision=precise_mode)

def long_conv(product, rates, coefs):
    groups = rates.shape[0]
    pieces = product.reshape(N_CTX, TOK_CTX, groups, GROUP_CH)
    decay = jnp.exp(-jnp.transpose(rates) * TOK_CTX)[:, :, None]

    def advance(state, piece):
        local, state_here = local_terms(piece, rates, coefs)
        total = local + carry_terms(rates, coefs, state, TOK_CTX)
        return (decay * state + state_here, jnp.transpose(total, (1, 0, 2)))
    start = jnp.zeros((ORDER, groups, GROUP_CH), jnp.float32)
    unused, outputs = lax.scan(advance, start, pieces)
    return outputs.reshape(N_CTX * TOK_CTX, groups * GROUP_CH)

def reference(features, residual, short_weight, rates, residues, out_weight):
    length = features.shape[0]
    part = D // N_TP
    coefs_all = residues * jnp.sqrt(1.0 - jnp.exp(-2.0 * rates))

    def channel_block(index):
        first = index * part
        block = lax.dynamic_slice_in_dim(features, first, part, 2).astype(jnp.float32)
        taps = lax.dynamic_slice_in_dim(short_weight, first, part, 2)
        padded = jnp.concatenate([jnp.zeros((6, 3, part), jnp.float32), block], 0)
        short = taps[0] * padded[6:]
        for tap_index in range(1, 7):
            short = short + taps[tap_index] * padded[6 - tap_index:6 - tap_index + length]
        query = short[:, 0]
        product = (short[:, 1] * short[:, 2]).reshape(length, part // GROUP_CH, GROUP_CH)
        rate_blk = lax.dynamic_slice_in_dim(rates, index * (part // GROUP_CH), part // GROUP_CH, 0)
        coef_blk = lax.dynamic_slice_in_dim(coefs_all, index * (part // GROUP_CH), part // GROUP_CH, 0)
        longer = long_conv(product, rate_blk, coef_blk)
        return (query * longer).astype(jnp.bfloat16)
    blocks = lax.map(channel_block, jnp.arange(N_TP, dtype=jnp.int32))
    gated = jnp.transpose(blocks, (1, 0, 2)).reshape(length, D)

    def add_part(index, total):
        rows_in = lax.dynamic_slice_in_dim(gated, index * part, part, 1)
        weights = lax.dynamic_slice_in_dim(out_weight, index * part, part, 0)
        term = jnp.dot(rows_in, weights, preferred_element_type=jnp.float32).astype(jnp.bfloat16)
        term = lax.optimization_barrier(term)
        return total + term.astype(jnp.float32)
    summed = lax.fori_loop(0, N_TP, add_part, jnp.zeros((length, D), jnp.float32))
    return (residual.astype(jnp.float32) + summed).astype(jnp.bfloat16)
```

```python
import functools

import jax
import jax.numpy as jnp
from jax import lax
from jax.experimental import pallas as pl
from jax.experimental.pallas import tpu as pltpu
from jax.sharding import PartitionSpec as P

MESH = pl.DeviceIdType.MESH
BF16 = jnp.bfloat16
F32 = jnp.float32
HIGHEST = lax.Precision.HIGHEST

GROUP_CH = 16
MINOR = 4
HALO = 16
TAPS = 7
SUB = 128
ROWS_STEP = 64
COLS = 1024
FAR, NEAR = 4, 3


def iota(shape, dim):
    return lax.broadcasted_iota(jnp.int32, shape, dim)


def split(value):
    high = value.astype(BF16)
    return high, (value - high.astype(F32)).astype(BF16)


def dot(a, b):
    return jnp.dot(a, b, preferred_element_type=F32)


def dot3(a, b):
    return dot(a[0], b[0]) + dot(a[0], b[1]) + dot(a[1], b[0])


def over_groups(table, picks):
    return lax.dot_general(
        table, picks, (((0,), (0,)), ((), ())), precision=HIGHEST, preferred_element_type=F32
    )


def kernel(
    n_ctx,
    n_tp,
    feat,
    resid,
    taps,
    rates,
    residues,
    weight,
    out,
    block,
    wide,
    product,
    query,
    local,
    toeplitz,
    masked,
    inward,
    gated,
    sibling,
    w_own,
    w_sib,
    part,
    going,
    coming,
    res_in,
    x_all,
    z_all,
    load_sem,
    kv_send,
    kv_recv,
    q_send,
    q_recv,
    edge_send,
    edge_recv,
    x_send,
    x_recv,
    z_send,
    z_recv,
    pair_send,
    pair_recv,
    ring_send,
    ring_recv,
):
    ctx = lax.axis_index("ctx")
    tp = lax.axis_index("tp")
    n_z = n_ctx // MINOR
    n_y = n_tp // 2
    z, x = lax.div(ctx, MINOR), lax.rem(ctx, MINOR)
    y, core = lax.div(tp, 2), lax.rem(tp, 2)
    other = (ctx, 2 * y + 1 - core)
    rows = feat.shape[1]
    channels = taps.shape[2]
    groups, order = rates.shape
    poles = groups * order
    length = n_tp * rows
    subs = length // SUB
    pieces = out.shape[1] // COLS

    def tp_at(step):
        return lax.rem(tp + step, n_tp)

    def x_at(step):
        return z * MINOR + lax.rem(x + step, MINOR)

    def z_at(step):
        return lax.rem(z + step, n_z) * MINOR + x

    nxt = lax.rem(ctx + 1, n_ctx)
    prv = lax.rem(ctx + n_ctx - 1, n_ctx)

    load_w = pltpu.make_async_copy(weight, w_own, load_sem.at[0])
    load_r = pltpu.make_async_copy(resid, res_in, load_sem.at[1])

    def columns(i):
        return pl.ds(pl.multiple_of(i * channels, channels), channels)

    def block_rows(i):
        return pl.ds(pl.multiple_of(HALO + i * rows, HALO), rows)

    own_kv = pltpu.make_async_copy(
        feat.at[pl.ds(1, 2), :, columns(tp)], block.at[pl.ds(1, 2), block_rows(tp), :], kv_recv.at[tp]
    )
    own_q = pltpu.make_async_copy(
        feat.at[pl.ds(0, 1), :, columns(tp)], block.at[pl.ds(0, 1), block_rows(tp), :], q_recv.at[tp]
    )
    own_kv.start()
    own_q.start()
    load_w.start()
    load_r.start()

    barrier = pltpu.get_barrier_semaphore()

    def greet(device):
        pl.semaphore_signal(barrier, inc=1, device_id=device, device_id_type=MESH)

    @pl.loop(1, n_tp)
    def _(step):
        greet((ctx, tp_at(step)))

    @pl.loop(1, MINOR)
    def _(step):
        greet((x_at(step), tp))

    @pl.loop(1, n_z)
    def _(step):
        greet((z_at(step), tp))

    greet((prv, tp))
    pl.semaphore_wait(barrier, n_tp - 1 + MINOR - 1 + n_z - 1 + 1)

    def send_branch(first, count, step, send_sem, recv_sem):
        to = tp_at(step)
        return pltpu.make_async_remote_copy(
            src_ref=feat.at[pl.ds(first, count), :, columns(to)],
            dst_ref=block.at[pl.ds(first, count), block_rows(tp), :],
            send_sem=send_sem.at[to],
            recv_sem=recv_sem.at[tp],
            device_id=(ctx, to),
            device_id_type=MESH,
        )

    @pl.loop(1, n_tp)
    def _(step):
        send_branch(1, 2, step, kv_send, kv_recv).start()

    send_w = pltpu.make_async_remote_copy(
        src_ref=weight,
        dst_ref=w_sib,
        send_sem=pair_send.at[0],
        recv_sem=pair_recv.at[0],
        device_id=other,
        device_id_type=MESH,
    )
    send_w.start()

    rate = rates[...]
    coef = residues[...] * jnp.sqrt(1.0 - jnp.exp(-2.0 * rate))
    pick_pole = (iota((groups, poles), 1) // order == iota((groups, poles), 0)).astype(F32)
    same_row = iota((order, poles), 1) % order == iota((order, poles), 0)
    rate_row = jnp.sum(jnp.where(same_row, over_groups(rate, pick_pole), 0.0), axis=0, keepdims=True)
    coef_row = jnp.sum(jnp.where(same_row, over_groups(coef, pick_pole), 0.0), axis=0, keepdims=True)
    pick_group = (iota((poles, groups), 0) // order == iota((poles, groups), 1)).astype(F32)
    same_col = iota((poles, order), 0) % order == iota((poles, order), 1)
    rate_col = jnp.sum(
        jnp.where(same_col, jnp.dot(pick_group, rate, precision=HIGHEST, preferred_element_type=F32), 0.0),
        axis=1,
        keepdims=True,
    )
    pick_channel = (iota((groups, channels), 1) // GROUP_CH == iota((groups, channels), 0)).astype(F32)
    rate_ch = over_groups(rate, pick_channel)
    decay_sub = jnp.exp(-rate_ch * SUB)
    decay = jnp.exp(-rate_ch * length)
    matching = iota((poles, channels), 0) // order == iota((poles, channels), 1) // GROUP_CH

    place = iota((SUB, poles), 0).astype(F32)
    falling = split(coef_row * jnp.exp(-rate_row * place))
    place = iota((poles, SUB), 1).astype(F32)
    rising = split(jnp.exp(rate_col * place))
    outof = split(jnp.exp(-rate_col * (SUB - 1.0 - place)))
    for b in range(subs):
        rows_b = pl.ds(b * SUB, SUB)
        place = (iota((SUB, poles), 0) + (b * SUB + 1)).astype(F32)
        high, low = split(coef_row * jnp.exp(-rate_row * place))
        inward[0, rows_b, :] = high
        inward[1, rows_b, :] = low
    causal = iota((SUB, SUB), 0) >= iota((SUB, SUB), 1)
    pole_group = iota((poles, SUB), 0) // order
    zero = jnp.zeros((), BF16)
    for g in range(groups):
        mine = pole_group == g
        part_g = (jnp.where(mine, rising[0], zero), jnp.where(mine, rising[1], zero))
        toeplitz[:, g * SUB : (g + 1) * SUB] = jnp.where(causal, dot3(falling, part_g), 0.0).astype(BF16)

    def await_rows(first, count, i, sem):
        piece = block.at[pl.ds(first, count), block_rows(i), :]
        pltpu.make_async_copy(piece, piece, sem.at[i]).wait()

    def send_edge(first, count, i):
        return pltpu.make_async_remote_copy(
            src_ref=block.at[pl.ds(first, count), pl.ds(length, HALO), :],
            dst_ref=block.at[pl.ds(first, count), pl.ds(0, HALO), :],
            send_sem=edge_send.at[i],
            recv_sem=edge_recv.at[i],
            device_id=(nxt, tp),
            device_id_type=MESH,
        )

    await_rows(1, 2, n_tp - 1, kv_recv)
    kv_edge = send_edge(1, 2, 0)
    kv_edge.start()

    @pl.loop(1, n_tp)
    def _(step):
        send_branch(1, 2, step, kv_send, kv_recv).wait_send()

    @pl.loop(1, n_tp)
    def _(step):
        send_branch(0, 1, step, q_send, q_recv).start()

    @pl.loop(0, n_tp - 1)
    def _(i):
        await_rows(1, 2, i, kv_recv)

    kv_edge.wait_recv()

    def widen(branch, slot):
        edge = block[branch, 0:HALO, :].astype(F32)
        wide[slot, 0:HALO, :] = jnp.where(ctx == 0, jnp.zeros_like(edge), edge)
        for start in range(0, length, SUB):
            wide[slot, HALO + start : HALO + start + SUB, :] = block[
                branch, HALO + start : HALO + start + SUB, :
            ].astype(F32)

    def short_conv(branch, slot, start):
        total = taps[branch, 0:1, :] * wide[slot, HALO + start : HALO + start + ROWS_STEP, :]
        for j in range(1, TAPS):
            total = total + taps[branch, j : j + 1, :] * wide[
                slot, HALO + start - j : HALO + start - j + ROWS_STEP, :
            ]
        return total

    widen(1, 0)
    widen(2, 1)
    state = jnp.zeros((order, channels), F32)
    before = []
    for b in range(subs):
        for start in range(b * SUB, (b + 1) * SUB, ROWS_STEP):
            product[start : start + ROWS_STEP, :] = short_conv(1, 0, start) * short_conv(2, 1, start)
        spread = dot3(outof, split(product[b * SUB : (b + 1) * SUB, :]))
        spread = jnp.where(matching, spread, 0.0).reshape(groups, order, channels)
        before.append(state)
        state = decay_sub * state + jnp.sum(spread, axis=0)

    x_all[x] = state

    def send_x(step):
        return pltpu.make_async_remote_copy(
            src_ref=x_all.at[x],
            dst_ref=x_all.at[x],
            send_sem=x_send.at[step],
            recv_sem=x_recv.at[x],
            device_id=(x_at(step), tp),
            device_id_type=MESH,
        )

    for step in range(1, MINOR):
        send_x(step).start()

    def expand(value):
        tiled = jnp.broadcast_to(value[None], (groups, order, channels)).reshape(poles, channels)
        return split(jnp.where(matching, tiled, 0.0))

    channel_group = iota((SUB, channels), 1) // GROUP_CH

    def local_sub(b):
        values = product[b * SUB : (b + 1) * SUB, :].astype(BF16)
        for g in range(groups):
            masked[g * SUB : (g + 1) * SUB, :] = jnp.where(channel_group == g, values, zero)
        total = dot(toeplitz[...], masked[...])
        if b > 0:
            total = total + dot3((inward[0, 0:SUB, :], inward[1, 0:SUB, :]), expand(before[b]))
        local[b * SUB : (b + 1) * SUB, :] = total

    local_sub(0)
    local_sub(1)

    for step in range(1, MINOR):
        i = lax.rem(x + step, MINOR)
        pltpu.make_async_copy(x_all.at[i], x_all.at[i], x_recv.at[i]).wait()
    row_total = x_all[0]
    row_before = jnp.zeros_like(row_total)
    for i in range(MINOR):
        if i > 0:
            row_total = decay * row_total + x_all[i]
        row_before = jnp.where(x > i, decay * row_before + x_all[i], row_before)

    z_all[z] = row_total

    def send_z(step):
        return pltpu.make_async_remote_copy(
            src_ref=z_all.at[z],
            dst_ref=z_all.at[z],
            send_sem=z_send.at[step],
            recv_sem=z_recv.at[z],
            device_id=(z_at(step), tp),
            device_id_type=MESH,
        )

    for step in range(1, n_z):
        send_z(step).start()

    await_rows(0, 1, n_tp - 1, q_recv)
    q_edge = send_edge(0, 1, 1)
    q_edge.start()
    for b in range(2, subs):
        local_sub(b)

    @pl.loop(0, n_tp - 1)
    def _(i):
        await_rows(0, 1, i, q_recv)

    q_edge.wait_recv()
    widen(0, 0)
    for start in range(0, length, ROWS_STEP):
        query[start : start + ROWS_STEP, :] = short_conv(0, 0, start)

    for step in range(1, n_z):
        i = lax.rem(z + step, n_z)
        pltpu.make_async_copy(z_all.at[i], z_all.at[i], z_recv.at[i]).wait()
    decay_row = jnp.exp(-rate_ch * (length * MINOR))
    above = jnp.zeros((order, channels), F32)
    for i in range(n_z):
        above = jnp.where(z > i, decay_row * above + z_all[i], above)
    incoming = row_before + jnp.exp(-rate_ch * (length * x).astype(F32)) * above

    carried = expand(incoming)
    for start in range(0, length, SUB):
        total = local[start : start + SUB, :] + dot3(
            (inward[0, start : start + SUB, :], inward[1, start : start + SUB, :]), carried
        )
        value = (query[start : start + SUB, :] * total).astype(BF16)
        per = SUB // (2 * rows)
        gated[start // (2 * rows) : start // (2 * rows) + per] = value.reshape(per, 2, rows, channels)

    send_g = pltpu.make_async_remote_copy(
        src_ref=gated.at[:, 1 - core],
        dst_ref=sibling,
        send_sem=pair_send.at[1],
        recv_sem=pair_recv.at[1],
        device_id=other,
        device_id_type=MESH,
    )
    send_g.start()
    load_w.wait()
    send_w.wait()
    send_g.wait()

    sign = 1 - 2 * core

    def y_at(step):
        return lax.rem(y + sign * step + n_y, n_y)

    def ring(k, piece):
        ahead = y_at(1) if k < FAR else y_at(-1)
        cols = pl.ds(pl.multiple_of(piece * COLS, COLS), COLS)
        return pltpu.make_async_remote_copy(
            src_ref=going.at[k, :, cols],
            dst_ref=coming.at[k, :, cols],
            send_sem=ring_send.at[k, piece],
            recv_sem=ring_recv.at[k, piece],
            device_id=(ctx, 2 * ahead + core),
            device_id_type=MESH,
        )

    def target(k):
        return y_at(FAR - k) if k < FAR else y_at(-(NEAR - (k - FAR)))

    own_rows = gated[:, core].reshape(n_y * rows, channels)
    sib_rows = sibling[...].reshape(n_y * rows, channels)

    @pl.loop(0, pieces)
    def _(piece):
        cols = pl.ds(pl.multiple_of(piece * COLS, COLS), COLS)
        total = dot(own_rows, w_own[:, cols]) + dot(sib_rows, w_sib[:, cols])
        part[:, :, cols] = total.reshape(n_y, rows, COLS)
        for k in (0, FAR):
            going[k, :, cols] = part[target(k), :, cols].astype(BF16)
            ring(k, piece).start()

    for turn in range(1, FAR):

        @pl.loop(0, pieces)
        def _(piece, turn=turn):
            cols = pl.ds(pl.multiple_of(piece * COLS, COLS), COLS)
            for k in (turn, FAR + turn):
                if k < FAR + NEAR:
                    ring(k - 1, piece).wait_recv()
                    going[k, :, cols] = (
                        part[target(k), :, cols] + coming[k - 1, :, cols].astype(F32)
                    ).astype(BF16)
                    ring(k, piece).start()

    load_r.wait()

    @pl.loop(0, pieces)
    def _(piece):
        cols = pl.ds(pl.multiple_of(piece * COLS, COLS), COLS)
        ring(FAR - 1, piece).wait_recv()
        ring(FAR + NEAR - 1, piece).wait_recv()
        total = part[y, :, cols] + coming[FAR - 1, :, cols].astype(F32)
        total = total + coming[FAR + NEAR - 1, :, cols].astype(F32)
        out[:, cols] = (res_in[:, cols].astype(F32) + total).astype(BF16)

    kv_edge.wait_send()
    q_edge.wait_send()

    @pl.loop(1, n_tp)
    def _(step):
        send_branch(0, 1, step, q_send, q_recv).wait_send()

    for step in range(1, MINOR):
        send_x(step).wait_send()
    for step in range(1, n_z):
        send_z(step).wait_send()

    @pl.loop(0, pieces)
    def _(piece):
        for k in range(FAR + NEAR):
            ring(k, piece).wait_send()


def body(n_ctx, n_tp, features, residual, short_weight, rates, residues, out_weight):
    feat = jnp.transpose(features, (1, 0, 2))
    taps = jnp.transpose(short_weight, (1, 0, 2))
    rows, width = residual.shape
    channels = taps.shape[2]
    groups, order = rates.shape
    poles = groups * order
    length = n_tp * rows
    n_y = n_tp // 2
    pieces = width // COLS
    slots = FAR + NEAR
    n_z = n_ctx // MINOR
    any_spec = pl.BlockSpec(memory_space=pltpu.MemorySpace.HBM)
    vmem_spec = pl.BlockSpec(memory_space=pltpu.VMEM)
    dma = pltpu.SemaphoreType.DMA
    return pl.pallas_call(
        functools.partial(kernel, n_ctx, n_tp),
        out_shape=jax.ShapeDtypeStruct((rows, width), BF16),
        in_specs=[any_spec, any_spec, vmem_spec, vmem_spec, vmem_spec, any_spec],
        out_specs=vmem_spec,
        scratch_shapes=[
            pltpu.VMEM((3, HALO + length, channels), BF16),
            pltpu.VMEM((2, HALO + length, channels), F32),
            pltpu.VMEM((length, channels), F32),
            pltpu.VMEM((length, channels), F32),
            pltpu.VMEM((length, channels), F32),
            pltpu.VMEM((SUB, groups * SUB), BF16),
            pltpu.VMEM((groups * SUB, channels), BF16),
            pltpu.VMEM((2, length, poles), BF16),
            pltpu.VMEM((n_y, 2, rows, channels), BF16),
            pltpu.VMEM((n_y, rows, channels), BF16),
            pltpu.VMEM((channels, width), BF16),
            pltpu.VMEM((channels, width), BF16),
            pltpu.VMEM((n_y, rows, width), F32),
            pltpu.VMEM((slots, rows, width), BF16),
            pltpu.VMEM((slots, rows, width), BF16),
            pltpu.VMEM((rows, width), BF16),
            pltpu.VMEM((MINOR, order, channels), F32),
            pltpu.VMEM((n_z, order, channels), F32),
            dma((2,)),
            dma((n_tp,)),
            dma((n_tp,)),
            dma((n_tp,)),
            dma((n_tp,)),
            dma((2,)),
            dma((2,)),
            dma((MINOR,)),
            dma((MINOR,)),
            dma((n_z,)),
            dma((n_z,)),
            dma((2,)),
            dma((2,)),
            dma((slots, pieces)),
            dma((slots, pieces)),
        ],
        compiler_params=pltpu.CompilerParams(
            collective_id=0, has_side_effects=True, vmem_limit_bytes=48 * 1024 * 1024
        ),
    )(feat, residual, taps, rates, residues, out_weight)


def solution(mesh):
    in_specs = (
        P(("ctx", "tp"), None, None),
        P(("ctx", "tp"), None),
        P(None, None, "tp"),
        P("tp", None),
        P("tp", None),
        P("tp", None),
    )
    out_specs = P(("ctx", "tp"), None)
    run = functools.partial(body, mesh.shape["ctx"], mesh.shape["tp"])
    return jax.shard_map(run, mesh=mesh, in_specs=in_specs, out_specs=out_specs, check_vma=False)
```

```python
import functools

import jax
import jax.numpy as jnp
from jax import lax
from jax.experimental import pallas as pl
from jax.experimental.pallas import tpu as pltpu
from jax.sharding import PartitionSpec as P

MESH = pl.DeviceIdType.MESH
BF16 = jnp.bfloat16
F32 = jnp.float32
HIGHEST = lax.Precision.HIGHEST

GROUP_CH = 16
MINOR = 4
HALO = 16
TAPS = 7
SUB = 128
ROWS_STEP = 64
COLS = 1024
FAR, NEAR = 4, 3


def iota(shape, dim):
    return lax.broadcasted_iota(jnp.int32, shape, dim)


def split(value):
    high = value.astype(BF16)
    return high, (value - high.astype(F32)).astype(BF16)


def dot(a, b):
    return jnp.dot(a, b, preferred_element_type=F32)


def dot3(a, b):
    return dot(a[0], b[0]) + dot(a[0], b[1]) + dot(a[1], b[0])


def over_groups(table, picks):
    return lax.dot_general(
        table, picks, (((0,), (0,)), ((), ())), precision=HIGHEST, preferred_element_type=F32
    )


def kernel(
    n_ctx,
    n_tp,
    feat,
    resid,
    taps_in,
    rates_in,
    residues_in,
    weight,
    out,
    taps,
    rates,
    residues,
    block,
    wide,
    product,
    query,
    local,
    toeplitz,
    masked,
    inward,
    gated,
    sibling,
    w_own,
    w_sib,
    part,
    going,
    coming,
    res_in,
    x_all,
    z_all,
    load_sem,
    edge_ready,
    x_ready,
    z_ready,
    kv_send,
    kv_recv,
    q_send,
    q_recv,
    edge_send,
    edge_recv,
    x_send,
    x_recv,
    z_send,
    z_recv,
    pair_send,
    pair_recv,
    ring_send,
    ring_recv,
):
    ctx = lax.axis_index("ctx")
    tp = lax.axis_index("tp")
    n_z = n_ctx // MINOR
    n_y = n_tp // 2
    z, x = lax.div(ctx, MINOR), lax.rem(ctx, MINOR)
    y, core = lax.div(tp, 2), lax.rem(tp, 2)
    other = (ctx, 2 * y + 1 - core)
    rows = feat.shape[1]
    channels = taps_in.shape[2]
    groups, order = rates_in.shape
    poles = groups * order
    length = n_tp * rows
    subs = length // SUB
    pieces = out.shape[1] // COLS

    def tp_at(step):
        return lax.rem(tp + step, n_tp)

    def x_at(step):
        return z * MINOR + lax.rem(x + step, MINOR)

    nxt = lax.rem(ctx + 1, n_ctx)
    prv = lax.rem(ctx + n_ctx - 1, n_ctx)

    load_w = pltpu.make_async_copy(weight, w_own, load_sem.at[0])
    load_r = pltpu.make_async_copy(resid, res_in, load_sem.at[1])
    load_taps = pltpu.make_async_copy(taps_in, taps, load_sem.at[2])
    load_rates = pltpu.make_async_copy(rates_in, rates, load_sem.at[3])
    load_residues = pltpu.make_async_copy(residues_in, residues, load_sem.at[4])
    load_rates.start()
    load_residues.start()
    load_taps.start()

    last = (tp == n_tp - 1).astype(jnp.int32)

    def columns(i):
        return pl.ds(pl.multiple_of(i * channels, channels), channels)

    def block_rows(i):
        return pl.ds(pl.multiple_of(HALO + i * rows, HALO), rows)

    own_kv = pltpu.make_async_copy(
        feat.at[pl.ds(1, 2), :, columns(tp)], block.at[pl.ds(1, 2), block_rows(tp), :], kv_recv.at[last]
    )
    own_q = pltpu.make_async_copy(
        feat.at[pl.ds(0, 1), :, columns(tp)], block.at[pl.ds(0, 1), block_rows(tp), :], q_recv.at[last]
    )
    own_kv.start()
    own_q.start()
    load_w.start()
    load_r.start()

    @pl.when(ctx == 0)
    def _():
        block[:, 0:HALO, :] = jnp.zeros((3, HALO, channels), BF16)

    z_all[...] = jnp.zeros(z_all.shape, F32)

    barrier = pltpu.get_barrier_semaphore()

    def signal(sem, device):
        pl.semaphore_signal(sem, inc=1, device_id=device, device_id_type=MESH)

    @pl.loop(1, n_tp)
    def _(step):
        signal(barrier, (ctx, tp_at(step)))

    @pl.when(ctx < n_ctx - 1)
    def _():
        signal(barrier, (nxt, tp))

    for i in range(1, MINOR):

        @pl.when(x < i)
        def _(i=i):
            signal(barrier, (z * MINOR + i, tp))

    for i in range(1, n_z):

        @pl.when(z < i)
        def _(i=i):
            signal(barrier, (i * MINOR + x, tp))

    pl.semaphore_wait(barrier, n_tp - 1 + x + z + (ctx > 0).astype(jnp.int32))

    def send_branch(first, count, to, send_sem, recv_sem):
        return pltpu.make_async_remote_copy(
            src_ref=feat.at[pl.ds(first, count), :, columns(to)],
            dst_ref=block.at[pl.ds(first, count), block_rows(tp), :],
            send_sem=send_sem,
            recv_sem=recv_sem.at[last],
            device_id=(ctx, to),
            device_id_type=MESH,
        )

    def await_bytes(ref, sem):
        pltpu.make_async_copy(ref, ref, sem).wait()

    def others(first, count):
        return block.at[pl.ds(first, count), pl.ds(HALO, length - rows), :]

    half = n_y // 2
    ways = [(half, 1), (half, 0)]
    for dy in range(half - 1, 0, -1):
        ways += [(-dy, 1), (dy, 1), (-dy, 0), (dy, 0)]
    ways += [(0, 1)]

    def to_way(dy, swap):
        return 2 * lax.rem(y + dy + n_y, n_y) + (1 - core if swap else core)

    for way in ways:
        send_branch(1, 2, to_way(*way), kv_send, kv_recv).start()

    send_w = pltpu.make_async_remote_copy(
        src_ref=weight,
        dst_ref=w_sib,
        send_sem=pair_send.at[0],
        recv_sem=pair_recv.at[0],
        device_id=other,
        device_id_type=MESH,
    )
    send_w.start()

    for i in range(MINOR - 1):

        @pl.when(i < x)
        def _(i=i):
            signal(x_ready, (z * MINOR + i, tp))

    for i in range(n_z - 1):

        @pl.when(i < z)
        def _(i=i):
            signal(z_ready, (i * MINOR + x, tp))

    @pl.when(ctx > 0)
    def _():
        signal(edge_ready, (prv, tp))

    load_rates.wait()
    load_residues.wait()
    rate = rates[...]
    coef = residues[...] * jnp.sqrt(1.0 - jnp.exp(-2.0 * rate))
    pick_pole = (iota((groups, poles), 1) // order == iota((groups, poles), 0)).astype(F32)
    same_row = iota((order, poles), 1) % order == iota((order, poles), 0)
    rate_row = jnp.sum(jnp.where(same_row, over_groups(rate, pick_pole), 0.0), axis=0, keepdims=True)
    coef_row = jnp.sum(jnp.where(same_row, over_groups(coef, pick_pole), 0.0), axis=0, keepdims=True)
    pick_group = (iota((poles, groups), 0) // order == iota((poles, groups), 1)).astype(F32)
    same_col = iota((poles, order), 0) % order == iota((poles, order), 1)
    rate_col = jnp.sum(
        jnp.where(same_col, jnp.dot(pick_group, rate, precision=HIGHEST, preferred_element_type=F32), 0.0),
        axis=1,
        keepdims=True,
    )
    pick_channel = (iota((groups, channels), 1) // GROUP_CH == iota((groups, channels), 0)).astype(F32)
    rate_ch = over_groups(rate, pick_channel)
    decay_sub = jnp.exp(-rate_ch * SUB)
    decay = jnp.exp(-rate_ch * length)
    matching = iota((poles, channels), 0) // order == iota((poles, channels), 1) // GROUP_CH

    place = iota((SUB, poles), 0).astype(F32)
    falling = split(coef_row * jnp.exp(-rate_row * place))
    place = iota((poles, SUB), 1).astype(F32)
    rising = split(jnp.exp(rate_col * place))
    outof = split(jnp.exp(-rate_col * (SUB - 1.0 - place)))
    for b in range(subs):
        rows_b = pl.ds(b * SUB, SUB)
        place = (iota((SUB, poles), 0) + (b * SUB + 1)).astype(F32)
        high, low = split(coef_row * jnp.exp(-rate_row * place))
        inward[0, rows_b, :] = high
        inward[1, rows_b, :] = low
    causal = iota((SUB, SUB), 0) >= iota((SUB, SUB), 1)
    pole_group = iota((poles, SUB), 0) // order
    zero = jnp.zeros((), BF16)
    for g in range(groups):
        mine = pole_group == g
        part_g = (jnp.where(mine, rising[0], zero), jnp.where(mine, rising[1], zero))
        toeplitz[:, g * SUB : (g + 1) * SUB] = jnp.where(causal, dot3(falling, part_g), 0.0).astype(BF16)

    def send_edge(first, count, i):
        return pltpu.make_async_remote_copy(
            src_ref=block.at[pl.ds(first, count), pl.ds(length, HALO), :],
            dst_ref=block.at[pl.ds(first, count), pl.ds(0, HALO), :],
            send_sem=edge_send.at[i],
            recv_sem=edge_recv.at[i],
            device_id=(nxt, tp),
            device_id_type=MESH,
        )

    await_bytes(block.at[pl.ds(1, 2), block_rows(n_tp - 1), :], kv_recv.at[1])
    kv_edge = send_edge(1, 2, 0)

    @pl.when(ctx < n_ctx - 1)
    def _():
        pl.semaphore_wait(edge_ready, 1)
        kv_edge.start()

    await_bytes(others(1, 2), kv_send)
    for way in ways:
        send_branch(0, 1, to_way(*way), q_send, q_recv).start()

    await_bytes(others(1, 2), kv_recv.at[0])

    @pl.when(ctx > 0)
    def _():
        kv_edge.wait_recv()

    def widen(branch, slot):
        wide[slot, 0:HALO, :] = block[branch, 0:HALO, :].astype(F32)
        for start in range(0, length, SUB):
            wide[slot, HALO + start : HALO + start + SUB, :] = block[
                branch, HALO + start : HALO + start + SUB, :
            ].astype(F32)

    def short_conv(branch, slot, start):
        total = taps[branch, 0:1, :] * wide[slot, HALO + start : HALO + start + ROWS_STEP, :]
        for j in range(1, TAPS):
            total = total + taps[branch, j : j + 1, :] * wide[
                slot, HALO + start - j : HALO + start - j + ROWS_STEP, :
            ]
        return total

    load_taps.wait()
    widen(1, 0)
    widen(2, 1)
    state = jnp.zeros((order, channels), F32)
    before = []
    for b in range(subs):
        for start in range(b * SUB, (b + 1) * SUB, ROWS_STEP):
            product[start : start + ROWS_STEP, :] = short_conv(1, 0, start) * short_conv(2, 1, start)
        spread = dot3(outof, split(product[b * SUB : (b + 1) * SUB, :]))
        spread = jnp.where(matching, spread, 0.0).reshape(groups, order, channels)
        before.append(state)
        state = decay_sub * state + jnp.sum(spread, axis=0)

    x_all[x] = state

    def send_x(step):
        return pltpu.make_async_remote_copy(
            src_ref=x_all.at[x],
            dst_ref=x_all.at[x],
            send_sem=x_send,
            recv_sem=x_recv,
            device_id=(x_at(step), tp),
            device_id_type=MESH,
        )

    @pl.when(x < MINOR - 1)
    def _():
        pl.semaphore_wait(x_ready, MINOR - 1 - x)

    for step in range(1, MINOR):
        send_x(step).start()

    def expand(value):
        tiled = jnp.broadcast_to(value[None], (groups, order, channels)).reshape(poles, channels)
        return split(jnp.where(matching, tiled, 0.0))

    channel_group = iota((SUB, channels), 1) // GROUP_CH

    def local_sub(b):
        values = product[b * SUB : (b + 1) * SUB, :].astype(BF16)
        for g in range(groups):
            masked[g * SUB : (g + 1) * SUB, :] = jnp.where(channel_group == g, values, zero)
        total = dot(toeplitz[...], masked[...])
        if b > 0:
            total = total + dot3((inward[0, 0:SUB, :], inward[1, 0:SUB, :]), expand(before[b]))
        local[b * SUB : (b + 1) * SUB, :] = total

    local_sub(0)
    local_sub(1)

    await_bytes(x_all.at[pl.ds(0, MINOR - 1)], x_recv)
    row_total = x_all[0]
    row_before = jnp.zeros_like(row_total)
    for i in range(MINOR):
        if i > 0:
            row_total = decay * row_total + x_all[i]
        row_before = jnp.where(x > i, decay * row_before + x_all[i], row_before)

    z_all[z] = row_total

    def send_z(i):
        return pltpu.make_async_remote_copy(
            src_ref=z_all.at[z],
            dst_ref=z_all.at[z],
            send_sem=z_send.at[i],
            recv_sem=z_recv.at[z],
            device_id=(i * MINOR + x, tp),
            device_id_type=MESH,
        )

    @pl.when(z < n_z - 1)
    def _():
        pl.semaphore_wait(z_ready, n_z - 1 - z)

    for i in range(1, n_z):

        @pl.when(z < i)
        def _(i=i):
            send_z(i).start()

    q_edge = send_edge(0, 1, 1)
    await_bytes(block.at[pl.ds(0, 1), block_rows(n_tp - 1), :], q_recv.at[1])

    @pl.when(ctx < n_ctx - 1)
    def _():
        q_edge.start()

    for b in range(2, subs):
        local_sub(b)

    await_bytes(others(0, 1), q_recv.at[0])

    @pl.when(ctx > 0)
    def _():
        q_edge.wait_recv()

    widen(0, 0)
    for start in range(0, length, ROWS_STEP):
        query[start : start + ROWS_STEP, :] = short_conv(0, 0, start)

    for i in range(n_z - 1):

        @pl.when(i < z)
        def _(i=i):
            await_bytes(z_all.at[i], z_recv.at[i])

    decay_row = jnp.exp(-rate_ch * (length * MINOR))
    above = jnp.zeros((order, channels), F32)
    for i in range(n_z):
        above = jnp.where(z > i, decay_row * above + z_all[i], above)
    incoming = row_before + jnp.exp(-rate_ch * (length * x).astype(F32)) * above

    per = SUB // (2 * rows)

    def send_gated(b):
        return pltpu.make_async_remote_copy(
            src_ref=gated.at[pl.ds(b * per, per), 1 - core],
            dst_ref=sibling.at[pl.ds(b * per, per)],
            send_sem=pair_send.at[1],
            recv_sem=pair_recv.at[1],
            device_id=other,
            device_id_type=MESH,
        )

    carried = expand(incoming)
    for b in range(subs):
        rows_b = pl.ds(b * SUB, SUB)
        total = local[rows_b, :] + dot3((inward[0, rows_b, :], inward[1, rows_b, :]), carried)
        value = (query[rows_b, :] * total).astype(BF16)
        gated[b * per : (b + 1) * per] = value.reshape(per, 2, rows, channels)
        send_gated(b).start()
    load_w.wait()
    send_w.wait()
    await_bytes(sibling, pair_send.at[1])
    await_bytes(sibling, pair_recv.at[1])

    sign = 1 - 2 * core

    def y_at(step):
        return lax.rem(y + sign * step + n_y, n_y)

    def ring(k, piece):
        ahead = y_at(1) if k < FAR else y_at(-1)
        cols = pl.ds(pl.multiple_of(piece * COLS, COLS), COLS)
        return pltpu.make_async_remote_copy(
            src_ref=going.at[k, :, cols],
            dst_ref=coming.at[k, :, cols],
            send_sem=ring_send,
            recv_sem=ring_recv.at[k, piece],
            device_id=(ctx, 2 * ahead + core),
            device_id_type=MESH,
        )

    def target(k):
        return y_at(FAR - k) if k < FAR else y_at(-(NEAR - (k - FAR)))

    own_rows = gated[:, core].reshape(n_y * rows, channels)
    sib_rows = sibling[...].reshape(n_y * rows, channels)

    @pl.loop(0, pieces)
    def _(piece):
        cols = pl.ds(pl.multiple_of(piece * COLS, COLS), COLS)
        total = dot(own_rows, w_own[:, cols]) + dot(sib_rows, w_sib[:, cols])
        part[:, :, cols] = total.reshape(n_y, rows, COLS)
        for k in (0, FAR):
            going[k, :, cols] = part[target(k), :, cols].astype(BF16)
            ring(k, piece).start()

    for hop in range(1, FAR):

        @pl.loop(0, pieces)
        def _(piece, hop=hop):
            cols = pl.ds(pl.multiple_of(piece * COLS, COLS), COLS)
            for k in (hop, FAR + hop):
                if k < FAR + NEAR:
                    ring(k - 1, piece).wait_recv()
                    going[k, :, cols] = (
                        part[target(k), :, cols] + coming[k - 1, :, cols].astype(F32)
                    ).astype(BF16)
                    ring(k, piece).start()

    load_r.wait()

    @pl.loop(0, pieces)
    def _(piece):
        cols = pl.ds(pl.multiple_of(piece * COLS, COLS), COLS)
        ring(FAR - 1, piece).wait_recv()
        ring(FAR + NEAR - 1, piece).wait_recv()
        total = part[y, :, cols] + coming[FAR - 1, :, cols].astype(F32)
        total = total + coming[FAR + NEAR - 1, :, cols].astype(F32)
        out[:, cols] = (res_in[:, cols].astype(F32) + total).astype(BF16)

    @pl.when(ctx < n_ctx - 1)
    def _():
        kv_edge.wait_send()
        q_edge.wait_send()

    await_bytes(others(0, 1), q_send)
    await_bytes(x_all.at[pl.ds(0, MINOR - 1)], x_send)
    for i in range(1, n_z):

        @pl.when(z < i)
        def _(i=i):
            send_z(i).wait_send()

    await_bytes(going, ring_send)


def body(n_ctx, n_tp, features, residual, short_weight, rates, residues, out_weight):
    feat = jnp.transpose(features, (1, 0, 2))
    taps = jnp.transpose(short_weight, (1, 0, 2))
    rows, width = residual.shape
    channels = taps.shape[2]
    groups, order = rates.shape
    poles = groups * order
    length = n_tp * rows
    n_y = n_tp // 2
    pieces = width // COLS
    slots = FAR + NEAR
    n_z = n_ctx // MINOR
    any_spec = pl.BlockSpec(memory_space=pltpu.MemorySpace.HBM)
    vmem_spec = pl.BlockSpec(memory_space=pltpu.VMEM)
    dma = pltpu.SemaphoreType.DMA
    regular = pltpu.SemaphoreType.REGULAR
    return pl.pallas_call(
        functools.partial(kernel, n_ctx, n_tp),
        out_shape=jax.ShapeDtypeStruct((rows, width), BF16),
        in_specs=[any_spec] * 6,
        out_specs=vmem_spec,
        scratch_shapes=[
            pltpu.VMEM((3, TAPS, channels), F32),
            pltpu.VMEM((groups, order), F32),
            pltpu.VMEM((groups, order), F32),
            pltpu.VMEM((3, HALO + length, channels), BF16),
            pltpu.VMEM((2, HALO + length, channels), F32),
            pltpu.VMEM((length, channels), F32),
            pltpu.VMEM((length, channels), F32),
            pltpu.VMEM((length, channels), F32),
            pltpu.VMEM((SUB, groups * SUB), BF16),
            pltpu.VMEM((groups * SUB, channels), BF16),
            pltpu.VMEM((2, length, poles), BF16),
            pltpu.VMEM((n_y, 2, rows, channels), BF16),
            pltpu.VMEM((n_y, rows, channels), BF16),
            pltpu.VMEM((channels, width), BF16),
            pltpu.VMEM((channels, width), BF16),
            pltpu.VMEM((n_y, rows, width), F32),
            pltpu.VMEM((slots, rows, width), BF16),
            pltpu.VMEM((slots, rows, width), BF16),
            pltpu.VMEM((rows, width), BF16),
            pltpu.VMEM((MINOR, order, channels), F32),
            pltpu.VMEM((n_z, order, channels), F32),
            dma((5,)),
            regular,
            regular,
            regular,
            dma,
            dma((2,)),
            dma,
            dma((2,)),
            dma((2,)),
            dma((2,)),
            dma,
            dma,
            dma((n_z,)),
            dma((n_z,)),
            dma((2,)),
            dma((2,)),
            dma,
            dma((slots, pieces)),
        ],
        compiler_params=pltpu.CompilerParams(
            collective_id=0, has_side_effects=True, vmem_limit_bytes=60 * 1024 * 1024
        ),
    )(feat, residual, taps, rates, residues, out_weight)


def solution(mesh):
    in_specs = (
        P(("ctx", "tp"), None, None),
        P(("ctx", "tp"), None),
        P(None, None, "tp"),
        P("tp", None),
        P("tp", None),
        P("tp", None),
    )
    out_specs = P(("ctx", "tp"), None)
    run = functools.partial(body, mesh.shape["ctx"], mesh.shape["tp"])
    return jax.shard_map(run, mesh=mesh, in_specs=in_specs, out_specs=out_specs, check_vma=False)
```

```python
import functools

import jax
import jax.numpy as jnp
from jax import lax
from jax.experimental import pallas as pl
from jax.experimental.pallas import tpu as pltpu
from jax.sharding import PartitionSpec as P

MESH = pl.DeviceIdType.MESH
BF16 = jnp.bfloat16
F32 = jnp.float32
HIGHEST = lax.Precision.HIGHEST

GROUP_CH = 16
MINOR = 4
HALO = 16
TAPS = 7
SUB = 128
ROWS_STEP = 64
COLS = 1024
FAR, NEAR = 4, 3


def iota(shape, dim):
    return lax.broadcasted_iota(jnp.int32, shape, dim)


def split(value):
    high = value.astype(BF16)
    return high, (value - high.astype(F32)).astype(BF16)


def dot(a, b):
    return jnp.dot(a, b, preferred_element_type=F32)


def dot3(a, b):
    return dot(a[0], b[0]) + dot(a[0], b[1]) + dot(a[1], b[0])


def over_groups(table, picks):
    return lax.dot_general(
        table, picks, (((0,), (0,)), ((), ())), precision=HIGHEST, preferred_element_type=F32
    )


def kernel(
    n_ctx,
    n_tp,
    feat,
    resid,
    taps_in,
    rates_in,
    residues_in,
    weight,
    out,
    taps,
    rates,
    residues,
    block,
    wide,
    product,
    query,
    local,
    toeplitz,
    masked,
    inward,
    gated,
    sibling,
    w_own,
    w_sib,
    part,
    going,
    coming,
    res_in,
    x_all,
    z_all,
    load_sem,
    edge_ready,
    x_ready,
    z_ready,
    kv_send,
    kv_recv,
    q_send,
    q_recv,
    edge_send,
    edge_recv,
    x_send,
    x_recv,
    z_send,
    z_recv,
    pair_send,
    pair_recv,
    ring_send,
    ring_recv,
):
    ctx = lax.axis_index("ctx")
    tp = lax.axis_index("tp")
    n_z = n_ctx // MINOR
    n_y = n_tp // 2
    z, x = lax.div(ctx, MINOR), lax.rem(ctx, MINOR)
    y, core = lax.div(tp, 2), lax.rem(tp, 2)
    other = (ctx, 2 * y + 1 - core)
    rows = feat.shape[1]
    channels = taps_in.shape[2]
    groups, order = rates_in.shape
    poles = groups * order
    length = n_tp * rows
    subs = length // SUB
    pieces = out.shape[1] // COLS

    def tp_at(step):
        return lax.rem(tp + step, n_tp)

    def x_at(step):
        return z * MINOR + lax.rem(x + step, MINOR)

    nxt = lax.rem(ctx + 1, n_ctx)
    prv = lax.rem(ctx + n_ctx - 1, n_ctx)

    load_w = pltpu.make_async_copy(weight, w_own, load_sem.at[0])
    load_r = pltpu.make_async_copy(resid, res_in, load_sem.at[1])
    load_taps = pltpu.make_async_copy(taps_in, taps, load_sem.at[2])
    load_rates = pltpu.make_async_copy(rates_in, rates, load_sem.at[3])
    load_residues = pltpu.make_async_copy(residues_in, residues, load_sem.at[4])
    load_rates.start()
    load_residues.start()
    load_taps.start()

    last = (tp == n_tp - 1).astype(jnp.int32)

    def columns(i):
        return pl.ds(pl.multiple_of(i * channels, channels), channels)

    def block_rows(i):
        return pl.ds(pl.multiple_of(HALO + i * rows, HALO), rows)

    own_kv = pltpu.make_async_copy(
        feat.at[pl.ds(1, 2), :, columns(tp)], block.at[pl.ds(1, 2), block_rows(tp), :], kv_recv.at[last]
    )
    own_q = pltpu.make_async_copy(
        feat.at[pl.ds(0, 1), :, columns(tp)], block.at[pl.ds(0, 1), block_rows(tp), :], q_recv.at[last]
    )
    own_kv.start()
    own_q.start()
    load_w.start()
    load_r.start()

    @pl.when(ctx == 0)
    def _():
        block[:, 0:HALO, :] = jnp.zeros((3, HALO, channels), BF16)

    z_all[...] = jnp.zeros(z_all.shape, F32)

    barrier = pltpu.get_barrier_semaphore()

    def signal(sem, device):
        pl.semaphore_signal(sem, inc=1, device_id=device, device_id_type=MESH)

    @pl.loop(1, n_tp)
    def _(step):
        signal(barrier, (ctx, tp_at(step)))

    @pl.when(ctx < n_ctx - 1)
    def _():
        signal(barrier, (nxt, tp))

    for i in range(1, MINOR):

        @pl.when(x < i)
        def _(i=i):
            signal(barrier, (z * MINOR + i, tp))

    for i in range(1, n_z):

        @pl.when(z < i)
        def _(i=i):
            signal(barrier, (i * MINOR + x, tp))

    pl.semaphore_wait(barrier, n_tp - 1 + x + z + (ctx > 0).astype(jnp.int32))

    def send_branch(first, count, to, send_sem, recv_sem):
        return pltpu.make_async_remote_copy(
            src_ref=feat.at[pl.ds(first, count), :, columns(to)],
            dst_ref=block.at[pl.ds(first, count), block_rows(tp), :],
            send_sem=send_sem,
            recv_sem=recv_sem.at[last],
            device_id=(ctx, to),
            device_id_type=MESH,
        )

    def await_bytes(ref, sem):
        pltpu.make_async_copy(ref, ref, sem).wait()

    def others(first, count):
        return block.at[pl.ds(first, count), pl.ds(HALO, length - rows), :]

    half = n_y // 2
    ways = [(half, 1), (half, 0)]
    for dy in range(half - 1, 0, -1):
        ways += [(-dy, 1), (dy, 1), (-dy, 0), (dy, 0)]
    ways += [(0, 1)]

    def to_way(dy, swap):
        return 2 * lax.rem(y + dy + n_y, n_y) + (1 - core if swap else core)

    for way in ways:
        send_branch(1, 2, to_way(*way), kv_send, kv_recv).start()

    send_w = pltpu.make_async_remote_copy(
        src_ref=weight,
        dst_ref=w_sib,
        send_sem=pair_send.at[0],
        recv_sem=pair_recv.at[0],
        device_id=other,
        device_id_type=MESH,
    )
    send_w.start()

    for i in range(MINOR - 1):

        @pl.when(i < x)
        def _(i=i):
            signal(x_ready, (z * MINOR + i, tp))

    for i in range(n_z - 1):

        @pl.when(i < z)
        def _(i=i):
            signal(z_ready, (i * MINOR + x, tp))

    @pl.when(ctx > 0)
    def _():
        signal(edge_ready, (prv, tp))

    load_rates.wait()
    load_residues.wait()
    rate = rates[...]
    coef = residues[...] * jnp.sqrt(1.0 - jnp.exp(-2.0 * rate))
    pick_pole = (iota((groups, poles), 1) // order == iota((groups, poles), 0)).astype(F32)
    same_row = iota((order, poles), 1) % order == iota((order, poles), 0)
    rate_row = jnp.sum(jnp.where(same_row, over_groups(rate, pick_pole), 0.0), axis=0, keepdims=True)
    coef_row = jnp.sum(jnp.where(same_row, over_groups(coef, pick_pole), 0.0), axis=0, keepdims=True)
    pick_group = (iota((poles, groups), 0) // order == iota((poles, groups), 1)).astype(F32)
    same_col = iota((poles, order), 0) % order == iota((poles, order), 1)
    rate_col = jnp.sum(
        jnp.where(same_col, jnp.dot(pick_group, rate, precision=HIGHEST, preferred_element_type=F32), 0.0),
        axis=1,
        keepdims=True,
    )
    pick_channel = (iota((groups, channels), 1) // GROUP_CH == iota((groups, channels), 0)).astype(F32)
    rate_ch = over_groups(rate, pick_channel)
    decay_sub = jnp.exp(-rate_ch * SUB)
    decay = jnp.exp(-rate_ch * length)
    matching = iota((poles, channels), 0) // order == iota((poles, channels), 1) // GROUP_CH

    place = iota((SUB, poles), 0).astype(F32)
    falling = split(coef_row * jnp.exp(-rate_row * place))
    place = iota((poles, SUB), 1).astype(F32)
    rising = split(jnp.exp(rate_col * place))
    outof = split(jnp.exp(-rate_col * (SUB - 1.0 - place)))
    for b in range(subs):
        rows_b = pl.ds(b * SUB, SUB)
        place = (iota((SUB, poles), 0) + (b * SUB + 1)).astype(F32)
        high, low = split(coef_row * jnp.exp(-rate_row * place))
        inward[0, rows_b, :] = high
        inward[1, rows_b, :] = low
    causal = iota((SUB, SUB), 0) >= iota((SUB, SUB), 1)
    pole_group = iota((poles, SUB), 0) // order
    zero = jnp.zeros((), BF16)
    for g in range(groups):
        mine = pole_group == g
        part_g = (jnp.where(mine, rising[0], zero), jnp.where(mine, rising[1], zero))
        toeplitz[:, g * SUB : (g + 1) * SUB] = jnp.where(causal, dot3(falling, part_g), 0.0).astype(BF16)

    def send_edge(first, count, i):
        return pltpu.make_async_remote_copy(
            src_ref=block.at[pl.ds(first, count), pl.ds(length, HALO), :],
            dst_ref=block.at[pl.ds(first, count), pl.ds(0, HALO), :],
            send_sem=edge_send.at[i],
            recv_sem=edge_recv.at[i],
            device_id=(nxt, tp),
            device_id_type=MESH,
        )

    await_bytes(block.at[pl.ds(1, 2), block_rows(n_tp - 1), :], kv_recv.at[1])
    kv_edge = send_edge(1, 2, 0)

    @pl.when(ctx < n_ctx - 1)
    def _():
        pl.semaphore_wait(edge_ready, 1)
        kv_edge.start()

    await_bytes(others(1, 2), kv_send)
    for way in ways:
        send_branch(0, 1, to_way(*way), q_send, q_recv).start()

    await_bytes(others(1, 2), kv_recv.at[0])

    @pl.when(ctx > 0)
    def _():
        kv_edge.wait_recv()

    def widen(branch, slot):
        wide[slot, 0:HALO, :] = block[branch, 0:HALO, :].astype(F32)
        for start in range(0, length, SUB):
            wide[slot, HALO + start : HALO + start + SUB, :] = block[
                branch, HALO + start : HALO + start + SUB, :
            ].astype(F32)

    def short_conv(branch, slot, start):
        total = taps[branch, 0:1, :] * wide[slot, HALO + start : HALO + start + ROWS_STEP, :]
        for j in range(1, TAPS):
            total = total + taps[branch, j : j + 1, :] * wide[
                slot, HALO + start - j : HALO + start - j + ROWS_STEP, :
            ]
        return total

    load_taps.wait()
    widen(1, 0)
    widen(2, 1)
    state = jnp.zeros((order, channels), F32)
    before = []
    for b in range(subs):
        for start in range(b * SUB, (b + 1) * SUB, ROWS_STEP):
            product[start : start + ROWS_STEP, :] = short_conv(1, 0, start) * short_conv(2, 1, start)
        spread = dot3(outof, split(product[b * SUB : (b + 1) * SUB, :]))
        spread = jnp.where(matching, spread, 0.0).reshape(groups, order, channels)
        before.append(state)
        state = decay_sub * state + jnp.sum(spread, axis=0)

    x_all[x] = state

    def send_x(step):
        return pltpu.make_async_remote_copy(
            src_ref=x_all.at[x],
            dst_ref=x_all.at[x],
            send_sem=x_send,
            recv_sem=x_recv,
            device_id=(x_at(step), tp),
            device_id_type=MESH,
        )

    @pl.when(x < MINOR - 1)
    def _():
        pl.semaphore_wait(x_ready, MINOR - 1 - x)

    for step in range(1, MINOR):
        send_x(step).start()

    def expand(value):
        tiled = jnp.broadcast_to(value[None], (groups, order, channels)).reshape(poles, channels)
        return split(jnp.where(matching, tiled, 0.0))

    channel_group = iota((SUB, channels), 1) // GROUP_CH

    def local_sub(b):
        values = product[b * SUB : (b + 1) * SUB, :].astype(BF16)
        for g in range(groups):
            masked[g * SUB : (g + 1) * SUB, :] = jnp.where(channel_group == g, values, zero)
        total = dot(toeplitz[...], masked[...])
        if b > 0:
            total = total + dot3((inward[0, 0:SUB, :], inward[1, 0:SUB, :]), expand(before[b]))
        local[b * SUB : (b + 1) * SUB, :] = total

    local_sub(0)
    local_sub(1)

    await_bytes(x_all.at[pl.ds(0, MINOR - 1)], x_recv)
    row_total = x_all[0]
    row_before = jnp.zeros_like(row_total)
    for i in range(MINOR):
        if i > 0:
            row_total = decay * row_total + x_all[i]
        row_before = jnp.where(x > i, decay * row_before + x_all[i], row_before)

    z_all[z] = row_total

    def send_z(i):
        return pltpu.make_async_remote_copy(
            src_ref=z_all.at[z],
            dst_ref=z_all.at[z],
            send_sem=z_send.at[i],
            recv_sem=z_recv.at[z],
            device_id=(i * MINOR + x, tp),
            device_id_type=MESH,
        )

    @pl.when(z < n_z - 1)
    def _():
        pl.semaphore_wait(z_ready, n_z - 1 - z)

    for i in range(1, n_z):

        @pl.when(z < i)
        def _(i=i):
            send_z(i).start()

    q_edge = send_edge(0, 1, 1)
    await_bytes(block.at[pl.ds(0, 1), block_rows(n_tp - 1), :], q_recv.at[1])

    @pl.when(ctx < n_ctx - 1)
    def _():
        q_edge.start()

    for b in range(2, subs):
        local_sub(b)

    await_bytes(others(0, 1), q_recv.at[0])

    @pl.when(ctx > 0)
    def _():
        q_edge.wait_recv()

    widen(0, 0)
    for start in range(0, length, ROWS_STEP):
        query[start : start + ROWS_STEP, :] = short_conv(0, 0, start)

    for i in range(n_z - 1):

        @pl.when(i < z)
        def _(i=i):
            await_bytes(z_all.at[i], z_recv.at[i])

    decay_row = jnp.exp(-rate_ch * (length * MINOR))
    above = jnp.zeros((order, channels), F32)
    for i in range(n_z):
        above = jnp.where(z > i, decay_row * above + z_all[i], above)
    incoming = row_before + jnp.exp(-rate_ch * (length * x).astype(F32)) * above

    per = SUB // (2 * rows)

    def send_gated(b):
        return pltpu.make_async_remote_copy(
            src_ref=gated.at[pl.ds(b * per, per), 1 - core],
            dst_ref=sibling.at[pl.ds(b * per, per)],
            send_sem=pair_send.at[1],
            recv_sem=pair_recv.at[1],
            device_id=other,
            device_id_type=MESH,
        )

    carried = expand(incoming)
    for b in range(subs):
        rows_b = pl.ds(b * SUB, SUB)
        total = local[rows_b, :] + dot3((inward[0, rows_b, :], inward[1, rows_b, :]), carried)
        value = (query[rows_b, :] * total).astype(BF16)
        gated[b * per : (b + 1) * per] = value.reshape(per, 2, rows, channels)
        send_gated(b).start()
    load_w.wait()
    own_rows = gated[:, core].reshape(n_y * rows, channels)

    @pl.loop(0, pieces)
    def _(piece):
        cols = pl.ds(pl.multiple_of(piece * COLS, COLS), COLS)
        part[:, :, cols] = dot(own_rows, w_own[:, cols]).reshape(n_y, rows, COLS)

    send_w.wait()
    await_bytes(sibling, pair_send.at[1])
    await_bytes(sibling, pair_recv.at[1])

    sign = 1 - 2 * core

    def y_at(step):
        return lax.rem(y + sign * step + n_y, n_y)

    def ring(k, piece):
        ahead = y_at(1) if k < FAR else y_at(-1)
        cols = pl.ds(pl.multiple_of(piece * COLS, COLS), COLS)
        return pltpu.make_async_remote_copy(
            src_ref=going.at[k, :, cols],
            dst_ref=coming.at[k, :, cols],
            send_sem=ring_send,
            recv_sem=ring_recv.at[k, piece],
            device_id=(ctx, 2 * ahead + core),
            device_id_type=MESH,
        )

    def target(k):
        return y_at(FAR - k) if k < FAR else y_at(-(NEAR - (k - FAR)))

    sib_rows = sibling[...].reshape(n_y * rows, channels)

    @pl.loop(0, pieces)
    def _(piece):
        cols = pl.ds(pl.multiple_of(piece * COLS, COLS), COLS)
        part[:, :, cols] += dot(sib_rows, w_sib[:, cols]).reshape(n_y, rows, COLS)
        for k in (0, FAR):
            going[k, :, cols] = part[target(k), :, cols].astype(BF16)
            ring(k, piece).start()

    for hop in range(1, FAR):

        @pl.loop(0, pieces)
        def _(piece, hop=hop):
            cols = pl.ds(pl.multiple_of(piece * COLS, COLS), COLS)
            for k in (hop, FAR + hop):
                if k < FAR + NEAR:
                    ring(k - 1, piece).wait_recv()
                    going[k, :, cols] = (
                        part[target(k), :, cols] + coming[k - 1, :, cols].astype(F32)
                    ).astype(BF16)
                    ring(k, piece).start()

    load_r.wait()

    @pl.loop(0, pieces)
    def _(piece):
        cols = pl.ds(pl.multiple_of(piece * COLS, COLS), COLS)
        ring(FAR - 1, piece).wait_recv()
        ring(FAR + NEAR - 1, piece).wait_recv()
        total = part[y, :, cols] + coming[FAR - 1, :, cols].astype(F32)
        total = total + coming[FAR + NEAR - 1, :, cols].astype(F32)
        out[:, cols] = (res_in[:, cols].astype(F32) + total).astype(BF16)

    @pl.when(ctx < n_ctx - 1)
    def _():
        kv_edge.wait_send()
        q_edge.wait_send()

    await_bytes(others(0, 1), q_send)
    await_bytes(x_all.at[pl.ds(0, MINOR - 1)], x_send)
    for i in range(1, n_z):

        @pl.when(z < i)
        def _(i=i):
            send_z(i).wait_send()

    await_bytes(going, ring_send)


def body(n_ctx, n_tp, features, residual, short_weight, rates, residues, out_weight):
    feat = jnp.transpose(features, (1, 0, 2))
    taps = jnp.transpose(short_weight, (1, 0, 2))
    rows, width = residual.shape
    channels = taps.shape[2]
    groups, order = rates.shape
    poles = groups * order
    length = n_tp * rows
    n_y = n_tp // 2
    pieces = width // COLS
    slots = FAR + NEAR
    n_z = n_ctx // MINOR
    hbm = pltpu.MemorySpace.HBM
    any_spec = pl.BlockSpec(memory_space=hbm)
    args = (feat, residual, taps, rates, residues, out_weight)
    vmem_spec = pl.BlockSpec(memory_space=pltpu.VMEM)
    dma = pltpu.SemaphoreType.DMA
    regular = pltpu.SemaphoreType.REGULAR
    return pl.pallas_call(
        functools.partial(kernel, n_ctx, n_tp),
        out_shape=jax.ShapeDtypeStruct((rows, width), BF16),
        in_specs=[any_spec] * 6,
        out_specs=vmem_spec,
        scratch_shapes=[
            pltpu.VMEM((3, TAPS, channels), F32),
            pltpu.VMEM((groups, order), F32),
            pltpu.VMEM((groups, order), F32),
            pltpu.VMEM((3, HALO + length, channels), BF16),
            pltpu.VMEM((2, HALO + length, channels), F32),
            pltpu.VMEM((length, channels), F32),
            pltpu.VMEM((length, channels), F32),
            pltpu.VMEM((length, channels), F32),
            pltpu.VMEM((SUB, groups * SUB), BF16),
            pltpu.VMEM((groups * SUB, channels), BF16),
            pltpu.VMEM((2, length, poles), BF16),
            pltpu.VMEM((n_y, 2, rows, channels), BF16),
            pltpu.VMEM((n_y, rows, channels), BF16),
            pltpu.VMEM((channels, width), BF16),
            pltpu.VMEM((channels, width), BF16),
            pltpu.VMEM((n_y, rows, width), F32),
            pltpu.VMEM((slots, rows, width), BF16),
            pltpu.VMEM((slots, rows, width), BF16),
            pltpu.VMEM((rows, width), BF16),
            pltpu.VMEM((MINOR, order, channels), F32),
            pltpu.VMEM((n_z, order, channels), F32),
            dma((5,)),
            regular,
            regular,
            regular,
            dma,
            dma((2,)),
            dma,
            dma((2,)),
            dma((2,)),
            dma((2,)),
            dma,
            dma,
            dma((n_z,)),
            dma((n_z,)),
            dma((2,)),
            dma((2,)),
            dma,
            dma((slots, pieces)),
        ],
        compiler_params=pltpu.CompilerParams(
            collective_id=0, has_side_effects=True, vmem_limit_bytes=48 * 1024 * 1024
        ),
    )(*[pltpu.with_memory_space_constraint(arg, hbm) for arg in args])


def solution(mesh):
    in_specs = (
        P(("ctx", "tp"), None, None),
        P(("ctx", "tp"), None),
        P(None, None, "tp"),
        P("tp", None),
        P("tp", None),
        P("tp", None),
    )
    out_specs = P(("ctx", "tp"), None)
    run = functools.partial(body, mesh.shape["ctx"], mesh.shape["tp"])
    return jax.shard_map(run, mesh=mesh, in_specs=in_specs, out_specs=out_specs, check_vma=False)
```

```python
import functools

import jax
import jax.numpy as jnp
from jax import lax
from jax.experimental import pallas as pl
from jax.experimental.pallas import tpu as pltpu
from jax.sharding import PartitionSpec as P

MESH = pl.DeviceIdType.MESH
BF16 = jnp.bfloat16
F32 = jnp.float32
HIGHEST = lax.Precision.HIGHEST

GROUP_CH = 16
MINOR = 4
HALO = 16
TAPS = 7
SUB = 128
ROWS_STEP = 64
COLS = 1024
FAR, NEAR = 4, 3


def iota(shape, dim):
    return lax.broadcasted_iota(jnp.int32, shape, dim)


def split(value):
    high = value.astype(BF16)
    return high, (value - high.astype(F32)).astype(BF16)


def dot(a, b):
    return jnp.dot(a, b, preferred_element_type=F32)


def dot3(a, b):
    return dot(a[0], b[0]) + dot(a[0], b[1]) + dot(a[1], b[0])


def over_groups(table, picks):
    return lax.dot_general(
        table, picks, (((0,), (0,)), ((), ())), precision=HIGHEST, preferred_element_type=F32
    )


def kernel(
    n_ctx,
    n_tp,
    feat,
    resid,
    taps_in,
    rates_in,
    residues_in,
    weight,
    out,
    taps,
    rates,
    residues,
    block,
    wide,
    product,
    local,
    toeplitz,
    masked,
    inward,
    gated,
    sibling,
    w_own,
    w_sib,
    part,
    going,
    coming,
    res_in,
    x_all,
    z_all,
    load_sem,
    edge_ready,
    x_ready,
    z_ready,
    kv_send,
    kv_recv,
    q_send,
    q_recv,
    edge_send,
    edge_recv,
    x_send,
    x_recv,
    z_send,
    z_recv,
    pair_send,
    pair_recv,
    ring_send,
    ring_recv,
):
    ctx = lax.axis_index("ctx")
    tp = lax.axis_index("tp")
    n_z = n_ctx // MINOR
    n_y = n_tp // 2
    z, x = lax.div(ctx, MINOR), lax.rem(ctx, MINOR)
    y, core = lax.div(tp, 2), lax.rem(tp, 2)
    other = (ctx, 2 * y + 1 - core)
    rows = feat.shape[1]
    channels = taps_in.shape[2]
    groups, order = rates_in.shape
    poles = groups * order
    length = n_tp * rows
    subs = length // SUB
    pieces = out.shape[1] // COLS

    def tp_at(step):
        return lax.rem(tp + step, n_tp)

    def x_at(step):
        return z * MINOR + lax.rem(x + step, MINOR)

    nxt = lax.rem(ctx + 1, n_ctx)
    prv = lax.rem(ctx + n_ctx - 1, n_ctx)

    load_w = pltpu.make_async_copy(weight, w_own, load_sem.at[0])
    load_r = pltpu.make_async_copy(resid, res_in, load_sem.at[1])
    load_taps = pltpu.make_async_copy(taps_in, taps, load_sem.at[2])
    load_rates = pltpu.make_async_copy(rates_in, rates, load_sem.at[3])
    load_residues = pltpu.make_async_copy(residues_in, residues, load_sem.at[4])
    load_rates.start()
    load_residues.start()
    load_taps.start()

    last = (tp == n_tp - 1).astype(jnp.int32)

    def columns(i):
        return pl.ds(pl.multiple_of(i * channels, channels), channels)

    def block_rows(i):
        return pl.ds(pl.multiple_of(HALO + i * rows, HALO), rows)

    own_kv = pltpu.make_async_copy(
        feat.at[pl.ds(1, 2), :, columns(tp)], block.at[pl.ds(1, 2), block_rows(tp), :], kv_recv.at[last]
    )
    own_q = pltpu.make_async_copy(
        feat.at[pl.ds(0, 1), :, columns(tp)], block.at[pl.ds(0, 1), block_rows(tp), :], q_recv.at[last]
    )
    own_kv.start()
    own_q.start()
    load_w.start()
    load_r.start()

    @pl.when(ctx == 0)
    def _():
        block[:, 0:HALO, :] = jnp.zeros((3, HALO, channels), BF16)

    z_all[...] = jnp.zeros(z_all.shape, F32)

    barrier = pltpu.get_barrier_semaphore()

    def signal(sem, device):
        pl.semaphore_signal(sem, inc=1, device_id=device, device_id_type=MESH)

    @pl.loop(1, n_tp)
    def _(step):
        signal(barrier, (ctx, tp_at(step)))

    @pl.when(ctx < n_ctx - 1)
    def _():
        signal(barrier, (nxt, tp))

    for i in range(1, MINOR):

        @pl.when(x < i)
        def _(i=i):
            signal(barrier, (z * MINOR + i, tp))

    for i in range(1, n_z):

        @pl.when(z < i)
        def _(i=i):
            signal(barrier, (i * MINOR + x, tp))

    pl.semaphore_wait(barrier, n_tp - 1 + x + z + (ctx > 0).astype(jnp.int32))

    def send_branch(first, count, to, send_sem, recv_sem):
        return pltpu.make_async_remote_copy(
            src_ref=feat.at[pl.ds(first, count), :, columns(to)],
            dst_ref=block.at[pl.ds(first, count), block_rows(tp), :],
            send_sem=send_sem,
            recv_sem=recv_sem.at[last],
            device_id=(ctx, to),
            device_id_type=MESH,
        )

    def await_bytes(ref, sem):
        pltpu.make_async_copy(ref, ref, sem).wait()

    def others(first, count):
        return block.at[pl.ds(first, count), pl.ds(HALO, length - rows), :]

    half = n_y // 2
    ways = [(half, 1), (half, 0)]
    for dy in range(half - 1, 0, -1):
        ways += [(-dy, 1), (dy, 1), (-dy, 0), (dy, 0)]
    ways += [(0, 1)]

    def to_way(dy, swap):
        return 2 * lax.rem(y + dy + n_y, n_y) + (1 - core if swap else core)

    def send_queries():
        for way in ways:
            send_branch(0, 1, to_way(*way), q_send, q_recv).start()

    for way in ways:
        send_branch(1, 2, to_way(*way), kv_send, kv_recv).start()

    @pl.when(last == 1)
    def _():
        send_queries()


    for i in range(MINOR - 1):

        @pl.when(i < x)
        def _(i=i):
            signal(x_ready, (z * MINOR + i, tp))

    for i in range(n_z - 1):

        @pl.when(i < z)
        def _(i=i):
            signal(z_ready, (i * MINOR + x, tp))

    @pl.when(ctx > 0)
    def _():
        signal(edge_ready, (prv, tp))

    load_rates.wait()
    load_residues.wait()
    rate = rates[...]
    coef = residues[...] * jnp.sqrt(1.0 - jnp.exp(-2.0 * rate))
    pick_pole = (iota((groups, poles), 1) // order == iota((groups, poles), 0)).astype(F32)
    same_row = iota((order, poles), 1) % order == iota((order, poles), 0)
    rate_row = jnp.sum(jnp.where(same_row, over_groups(rate, pick_pole), 0.0), axis=0, keepdims=True)
    coef_row = jnp.sum(jnp.where(same_row, over_groups(coef, pick_pole), 0.0), axis=0, keepdims=True)
    pick_group = (iota((poles, groups), 0) // order == iota((poles, groups), 1)).astype(F32)
    same_col = iota((poles, order), 0) % order == iota((poles, order), 1)
    rate_col = jnp.sum(
        jnp.where(same_col, jnp.dot(pick_group, rate, precision=HIGHEST, preferred_element_type=F32), 0.0),
        axis=1,
        keepdims=True,
    )
    pick_channel = (iota((groups, channels), 1) // GROUP_CH == iota((groups, channels), 0)).astype(F32)
    rate_ch = over_groups(rate, pick_channel)
    decay_sub = jnp.exp(-rate_ch * SUB)
    decay = jnp.exp(-rate_ch * length)
    matching = iota((poles, channels), 0) // order == iota((poles, channels), 1) // GROUP_CH

    place = iota((SUB, poles), 0).astype(F32)
    falling = split(coef_row * jnp.exp(-rate_row * place))
    place = iota((poles, SUB), 1).astype(F32)
    rising = split(jnp.exp(rate_col * place))
    outof = split(jnp.exp(-rate_col * (SUB - 1.0 - place)))
    for b in range(subs):
        rows_b = pl.ds(b * SUB, SUB)
        place = (iota((SUB, poles), 0) + (b * SUB + 1)).astype(F32)
        high, low = split(coef_row * jnp.exp(-rate_row * place))
        inward[0, rows_b, :] = high
        inward[1, rows_b, :] = low
    causal = iota((SUB, SUB), 0) >= iota((SUB, SUB), 1)
    pole_group = iota((poles, SUB), 0) // order
    zero = jnp.zeros((), BF16)
    for g in range(groups):
        mine = pole_group == g
        part_g = (jnp.where(mine, rising[0], zero), jnp.where(mine, rising[1], zero))
        toeplitz[:, g * SUB : (g + 1) * SUB] = jnp.where(causal, dot3(falling, part_g), 0.0).astype(BF16)

    def send_edge(first, count, i):
        return pltpu.make_async_remote_copy(
            src_ref=block.at[pl.ds(first, count), pl.ds(length, HALO), :],
            dst_ref=block.at[pl.ds(first, count), pl.ds(0, HALO), :],
            send_sem=edge_send.at[i],
            recv_sem=edge_recv.at[i],
            device_id=(nxt, tp),
            device_id_type=MESH,
        )

    await_bytes(block.at[pl.ds(1, 2), block_rows(n_tp - 1), :], kv_recv.at[1])
    kv_edge = send_edge(1, 2, 0)

    @pl.when(ctx < n_ctx - 1)
    def _():
        pl.semaphore_wait(edge_ready, 1)
        kv_edge.start()

    await_bytes(others(1, 2), kv_send)

    @pl.when(last == 0)
    def _():
        send_queries()


    send_w = pltpu.make_async_remote_copy(
        src_ref=weight,
        dst_ref=w_sib,
        send_sem=pair_send.at[0],
        recv_sem=pair_recv.at[0],
        device_id=other,
        device_id_type=MESH,
    )
    send_w.start()


    await_bytes(others(1, 2), kv_recv.at[0])

    @pl.when(ctx > 0)
    def _():
        kv_edge.wait_recv()

    def widen(branch, slot):
        wide[slot, 0:HALO, :] = block[branch, 0:HALO, :].astype(F32)
        for start in range(0, length, SUB):
            wide[slot, HALO + start : HALO + start + SUB, :] = block[
                branch, HALO + start : HALO + start + SUB, :
            ].astype(F32)

    def short_conv(branch, rows_in, start):
        total = taps[branch, 0:1, :] * rows_in[HALO + start : HALO + start + ROWS_STEP, :]
        for j in range(1, TAPS):
            total = total + taps[branch, j : j + 1, :] * rows_in[HALO + start - j : HALO + start - j + ROWS_STEP, :]
        return total

    load_taps.wait()
    widen(1, 0)
    widen(2, 1)
    state = jnp.zeros((order, channels), F32)
    before = []
    for b in range(subs):
        for start in range(b * SUB, (b + 1) * SUB, ROWS_STEP):
            product[start : start + ROWS_STEP, :] = short_conv(1, wide.at[0], start) * short_conv(2, wide.at[1], start)
        spread = dot3(outof, split(product[b * SUB : (b + 1) * SUB, :]))
        spread = jnp.where(matching, spread, 0.0).reshape(groups, order, channels)
        before.append(state)
        state = decay_sub * state + jnp.sum(spread, axis=0)

    x_all[x] = state

    def send_x(step):
        return pltpu.make_async_remote_copy(
            src_ref=x_all.at[x],
            dst_ref=x_all.at[x],
            send_sem=x_send,
            recv_sem=x_recv,
            device_id=(x_at(step), tp),
            device_id_type=MESH,
        )

    @pl.when(x < MINOR - 1)
    def _():
        pl.semaphore_wait(x_ready, MINOR - 1 - x)

    for step in range(1, MINOR):
        send_x(step).start()

    def expand(value):
        tiled = jnp.broadcast_to(value[None], (groups, order, channels)).reshape(poles, channels)
        return split(jnp.where(matching, tiled, 0.0))

    channel_group = iota((SUB, channels), 1) // GROUP_CH

    def local_sub(b):
        values = product[b * SUB : (b + 1) * SUB, :].astype(BF16)
        for g in range(groups):
            masked[g * SUB : (g + 1) * SUB, :] = jnp.where(channel_group == g, values, zero)
        total = dot(toeplitz[...], masked[...])
        if b > 0:
            total = total + dot3((inward[0, 0:SUB, :], inward[1, 0:SUB, :]), expand(before[b]))
        local[b * SUB : (b + 1) * SUB, :] = total

    local_sub(0)
    local_sub(1)

    q_edge = send_edge(0, 1, 1)
    await_bytes(block.at[pl.ds(0, 1), block_rows(n_tp - 1), :], q_recv.at[1])

    @pl.when(ctx < n_ctx - 1)
    def _():
        q_edge.start()

    await_bytes(x_all.at[pl.ds(0, MINOR - 1)], x_recv)
    row_total = x_all[0]
    row_before = jnp.zeros_like(row_total)
    for i in range(MINOR):
        if i > 0:
            row_total = decay * row_total + x_all[i]
        row_before = jnp.where(x > i, decay * row_before + x_all[i], row_before)

    z_all[z] = row_total

    def send_z(i):
        return pltpu.make_async_remote_copy(
            src_ref=z_all.at[z],
            dst_ref=z_all.at[z],
            send_sem=z_send.at[i],
            recv_sem=z_recv.at[z],
            device_id=(i * MINOR + x, tp),
            device_id_type=MESH,
        )

    @pl.when(z < n_z - 1)
    def _():
        pl.semaphore_wait(z_ready, n_z - 1 - z)

    for i in range(1, n_z):

        @pl.when(z < i)
        def _(i=i):
            send_z(i).start()

    for b in range(2, subs):
        local_sub(b)

    await_bytes(others(0, 1), q_recv.at[0])

    @pl.when(ctx > 0)
    def _():
        q_edge.wait_recv()

    widen(0, 0)

    for i in range(n_z - 1):

        @pl.when(i < z)
        def _(i=i):
            await_bytes(z_all.at[i], z_recv.at[i])

    decay_row = jnp.exp(-rate_ch * (length * MINOR))
    above = jnp.zeros((order, channels), F32)
    for i in range(n_z):
        above = jnp.where(z > i, decay_row * above + z_all[i], above)
    incoming = row_before + jnp.exp(-rate_ch * (length * x).astype(F32)) * above

    per = SUB // (2 * rows)
    sign = 1 - 2 * core
    odd = 2 * lax.rem(y, 2) - 1
    first_sub = lax.div(lax.rem(y + n_y // 2, n_y), 2)
    order_subs = [lax.rem(first_sub + subs + odd * i, subs) for i in (0, 1, -1, 2)]

    def send_gated(b, i):
        return pltpu.make_async_remote_copy(
            src_ref=gated.at[pl.ds(b * per, per), 1 - core],
            dst_ref=sibling.at[pl.ds(b * per, per)],
            send_sem=pair_send.at[1],
            recv_sem=pair_recv.at[1 + i],
            device_id=other,
            device_id_type=MESH,
        )

    carried = expand(incoming)
    for i, b in enumerate(order_subs):
        rows_b = pl.ds(pl.multiple_of(b * SUB, SUB), SUB)
        total = local[rows_b, :] + dot3((inward[0, rows_b, :], inward[1, rows_b, :]), carried)
        rows_in = wide.at[0, pl.ds(pl.multiple_of(b * SUB, SUB), HALO + SUB), :]
        query = jnp.concatenate([short_conv(0, rows_in, start) for start in range(0, SUB, ROWS_STEP)], axis=0)
        value = (query * total).astype(BF16)
        gated[pl.ds(b * per, per)] = value.reshape(per, 2, rows, channels)
        send_gated(b, i // 2).start()

    def y_at(step):
        return lax.rem(y + sign * step + n_y, n_y)

    def ring(k, piece):
        ahead = y_at(1) if k < FAR else y_at(-1)
        cols = pl.ds(pl.multiple_of(piece * COLS, COLS), COLS)
        return pltpu.make_async_remote_copy(
            src_ref=going.at[k, :, cols],
            dst_ref=coming.at[k, :, cols],
            send_sem=ring_send,
            recv_sem=ring_recv.at[k, piece],
            device_id=(ctx, 2 * ahead + core),
            device_id_type=MESH,
        )

    def target(k):
        return y_at(FAR - k) if k < FAR else y_at(-(NEAR - (k - FAR)))

    def gather(chips):
        own = jnp.concatenate([gated[chip, core] for chip in chips], axis=0)
        return own, jnp.concatenate([sibling[chip] for chip in chips], axis=0)

    def project(pair, cols):
        return dot(pair[0], w_own[:, cols]) + dot(pair[1], w_sib[:, cols])

    half_bytes = sibling.at[pl.ds(0, n_y // 2)]
    load_w.wait()
    send_w.wait()
    await_bytes(half_bytes, pair_recv.at[1])
    leading = gather([target(0), target(FAR)])

    @pl.loop(0, pieces)
    def _(piece):
        cols = pl.ds(pl.multiple_of(piece * COLS, COLS), COLS)
        total = project(leading, cols).astype(BF16)
        for i, k in enumerate((0, FAR)):
            going[k, :, cols] = total[i * rows : (i + 1) * rows]
            ring(k, piece).start()

    later = [k for hop in range(1, FAR) for k in (hop, FAR + hop) if k < FAR + NEAR]
    await_bytes(half_bytes, pair_recv.at[2])
    following = gather([target(k) for k in later] + [y])

    @pl.loop(0, pieces)
    def _(piece):
        cols = pl.ds(pl.multiple_of(piece * COLS, COLS), COLS)
        part[:, :, cols] = project(following, cols).reshape(len(later) + 1, rows, COLS)

    for hop in range(1, FAR):

        @pl.loop(0, pieces)
        def _(piece, hop=hop):
            cols = pl.ds(pl.multiple_of(piece * COLS, COLS), COLS)
            for k in (hop, FAR + hop):
                if k < FAR + NEAR:
                    ring(k - 1, piece).wait_recv()
                    going[k, :, cols] = (
                        part[later.index(k), :, cols] + coming[k - 1, :, cols].astype(F32)
                    ).astype(BF16)
                    ring(k, piece).start()

    load_r.wait()

    @pl.loop(0, pieces)
    def _(piece):
        cols = pl.ds(pl.multiple_of(piece * COLS, COLS), COLS)
        ring(FAR - 1, piece).wait_recv()
        ring(FAR + NEAR - 1, piece).wait_recv()
        total = part[len(later), :, cols] + coming[FAR - 1, :, cols].astype(F32)
        total = total + coming[FAR + NEAR - 1, :, cols].astype(F32)
        out[:, cols] = (res_in[:, cols].astype(F32) + total).astype(BF16)

    @pl.when(ctx < n_ctx - 1)
    def _():
        kv_edge.wait_send()
        q_edge.wait_send()

    await_bytes(others(0, 1), q_send)
    await_bytes(x_all.at[pl.ds(0, MINOR - 1)], x_send)
    for i in range(1, n_z):

        @pl.when(z < i)
        def _(i=i):
            send_z(i).wait_send()

    await_bytes(sibling, pair_send.at[1])
    await_bytes(going, ring_send)


def body(n_ctx, n_tp, features, residual, short_weight, rates, residues, out_weight):
    feat = jnp.transpose(features, (1, 0, 2))
    taps = jnp.transpose(short_weight, (1, 0, 2))
    rows, width = residual.shape
    channels = taps.shape[2]
    groups, order = rates.shape
    poles = groups * order
    length = n_tp * rows
    n_y = n_tp // 2
    pieces = width // COLS
    slots = FAR + NEAR
    n_z = n_ctx // MINOR
    hbm = pltpu.MemorySpace.HBM
    any_spec = pl.BlockSpec(memory_space=hbm)
    args = (feat, residual, taps, rates, residues, out_weight)
    vmem_spec = pl.BlockSpec(memory_space=pltpu.VMEM)
    dma = pltpu.SemaphoreType.DMA
    regular = pltpu.SemaphoreType.REGULAR
    return pl.pallas_call(
        functools.partial(kernel, n_ctx, n_tp),
        out_shape=jax.ShapeDtypeStruct((rows, width), BF16),
        in_specs=[any_spec] * 6,
        out_specs=vmem_spec,
        scratch_shapes=[
            pltpu.VMEM((3, TAPS, channels), F32),
            pltpu.VMEM((groups, order), F32),
            pltpu.VMEM((groups, order), F32),
            pltpu.VMEM((3, HALO + length, channels), BF16),
            pltpu.VMEM((2, HALO + length, channels), F32),
            pltpu.VMEM((length, channels), F32),
            pltpu.VMEM((length, channels), F32),
            pltpu.VMEM((SUB, groups * SUB), BF16),
            pltpu.VMEM((groups * SUB, channels), BF16),
            pltpu.VMEM((2, length, poles), BF16),
            pltpu.VMEM((n_y, 2, rows, channels), BF16),
            pltpu.VMEM((n_y, rows, channels), BF16),
            pltpu.VMEM((channels, width), BF16),
            pltpu.VMEM((channels, width), BF16),
            pltpu.VMEM((slots - 1, rows, width), F32),
            pltpu.VMEM((slots, rows, width), BF16),
            pltpu.VMEM((slots, rows, width), BF16),
            pltpu.VMEM((rows, width), BF16),
            pltpu.VMEM((MINOR, order, channels), F32),
            pltpu.VMEM((n_z, order, channels), F32),
            dma((5,)),
            regular,
            regular,
            regular,
            dma,
            dma((2,)),
            dma,
            dma((2,)),
            dma((2,)),
            dma((2,)),
            dma,
            dma,
            dma((n_z,)),
            dma((n_z,)),
            dma((2,)),
            dma((3,)),
            dma,
            dma((slots, pieces)),
        ],
        compiler_params=pltpu.CompilerParams(
            collective_id=0, has_side_effects=True, vmem_limit_bytes=48 * 1024 * 1024
        ),
    )(*[pltpu.with_memory_space_constraint(arg, hbm) for arg in args])


def solution(mesh):
    in_specs = (
        P(("ctx", "tp"), None, None),
        P(("ctx", "tp"), None),
        P(None, None, "tp"),
        P("tp", None),
        P("tp", None),
        P("tp", None),
    )
    out_specs = P(("ctx", "tp"), None)
    run = functools.partial(body, mesh.shape["ctx"], mesh.shape["tp"])
    return jax.shard_map(run, mesh=mesh, in_specs=in_specs, out_specs=out_specs, check_vma=False)
```

```python
import functools

import jax
import jax.numpy as jnp
from jax import lax
from jax.experimental import pallas as pl
from jax.experimental.pallas import tpu as pltpu
from jax.sharding import PartitionSpec as P

MESH = pl.DeviceIdType.MESH
BF16 = jnp.bfloat16
F32 = jnp.float32
HIGHEST = lax.Precision.HIGHEST

GROUP_CH = 16
MINOR = 4
HALO = 16
TAPS = 7
SUB = 128
ROWS_STEP = 64
COLS = 1024
FAR, NEAR = 4, 3


def iota(shape, dim):
    return lax.broadcasted_iota(jnp.int32, shape, dim)


def split(value):
    high = value.astype(BF16)
    return high, (value - high.astype(F32)).astype(BF16)


def dot(a, b):
    return jnp.dot(a, b, preferred_element_type=F32)


def dot3(a, b):
    return dot(a[0], b[0]) + dot(a[0], b[1]) + dot(a[1], b[0])


def over_groups(table, picks):
    return lax.dot_general(
        table, picks, (((0,), (0,)), ((), ())), precision=HIGHEST, preferred_element_type=F32
    )


def kernel(
    n_ctx,
    n_tp,
    feat_in,
    resid,
    taps_in,
    rates_in,
    residues_in,
    weight,
    out,
    feat,
    taps,
    rates,
    residues,
    block,
    wide,
    product,
    local,
    toeplitz,
    masked,
    inward,
    gated,
    sibling,
    w_own,
    w_sib,
    part,
    going,
    coming,
    res_in,
    x_all,
    z_all,
    up_all,
    load_sem,
    edge_ready,
    x_ready,
    z_ready,
    up_ready,
    up_send,
    up_recv,
    kv_send,
    kv_recv,
    q_send,
    q_recv,
    edge_send,
    edge_recv,
    x_send,
    x_recv,
    z_send,
    z_recv,
    pair_send,
    pair_recv,
    ring_send,
    ring_recv,
):
    ctx = lax.axis_index("ctx")
    tp = lax.axis_index("tp")
    n_z = n_ctx // MINOR
    n_y = n_tp // 2
    z, x = lax.div(ctx, MINOR), lax.rem(ctx, MINOR)
    y, core = lax.div(tp, 2), lax.rem(tp, 2)
    other = (ctx, 2 * y + 1 - core)
    rows = feat_in.shape[1]
    channels = taps_in.shape[2]
    groups, order = rates_in.shape
    poles = groups * order
    length = n_tp * rows
    subs = length // SUB
    pieces = out.shape[1] // COLS

    def tp_at(step):
        return lax.rem(tp + step, n_tp)

    def x_at(step):
        return z * MINOR + lax.rem(x + step, MINOR)

    nxt = lax.rem(ctx + 1, n_ctx)
    prv = lax.rem(ctx + n_ctx - 1, n_ctx)

    barrier = pltpu.get_barrier_semaphore()

    def signal(sem, device):
        pl.semaphore_signal(sem, inc=1, device_id=device, device_id_type=MESH)

    for step in range(1, n_tp):
        signal(barrier, (ctx, tp_at(step)))

    load_kv = pltpu.make_async_copy(feat_in.at[pl.ds(1, 2)], feat.at[pl.ds(1, 2)], load_sem.at[5])
    load_q = pltpu.make_async_copy(feat_in.at[pl.ds(0, 1)], feat.at[pl.ds(0, 1)], load_sem.at[6])
    load_kv.start()
    load_q.start()
    load_w = pltpu.make_async_copy(weight, w_own, load_sem.at[0])
    load_r = pltpu.make_async_copy(resid, res_in, load_sem.at[1])
    load_taps = pltpu.make_async_copy(taps_in, taps, load_sem.at[2])
    load_rates = pltpu.make_async_copy(rates_in, rates, load_sem.at[3])
    load_residues = pltpu.make_async_copy(residues_in, residues, load_sem.at[4])
    load_rates.start()
    load_residues.start()
    load_taps.start()

    last = (tp == n_tp - 1).astype(jnp.int32)

    def columns(i):
        return pl.ds(pl.multiple_of(i * channels, channels), channels)

    def block_rows(i):
        return pl.ds(pl.multiple_of(HALO + i * rows, HALO), rows)

    own_kv = pltpu.make_async_copy(
        feat_in.at[pl.ds(1, 2), :, columns(tp)], block.at[pl.ds(1, 2), block_rows(tp), :], kv_recv.at[last]
    )
    own_q = pltpu.make_async_copy(
        feat_in.at[pl.ds(0, 1), :, columns(tp)], block.at[pl.ds(0, 1), block_rows(tp), :], q_recv.at[last]
    )
    own_kv.start()
    own_q.start()
    load_w.start()
    load_r.start()

    @pl.when(ctx == 0)
    def _():
        block[:, 0:HALO, :] = jnp.zeros((3, HALO, channels), BF16)

    z_all[...] = jnp.zeros(z_all.shape, F32)

    @pl.when(ctx < n_ctx - 1)
    def _():
        signal(barrier, (nxt, tp))

    for i in range(1, MINOR):

        @pl.when(x < i)
        def _(i=i):
            signal(barrier, (z * MINOR + i, tp))

    for i in range(1, n_z):

        @pl.when(z < i - 1)
        def _(i=i):
            signal(barrier, (i * MINOR + x, tp))

    @pl.when(z < n_z - 1)
    def _():
        for i in range(MINOR):
            signal(barrier, ((z + 1) * MINOR + i, tp))

    @pl.when(z == 0)
    def _():
        up_all[...] = jnp.zeros(up_all.shape, F32)

    load_kv.wait()
    up = (z > 0).astype(jnp.int32)
    pl.semaphore_wait(barrier, n_tp - 1 + x + z - up + MINOR * up + (ctx > 0).astype(jnp.int32))

    def send_branch(first, count, to, send_sem, recv_sem):
        return pltpu.make_async_remote_copy(
            src_ref=feat.at[pl.ds(first, count), :, columns(to)],
            dst_ref=block.at[pl.ds(first, count), block_rows(tp), :],
            send_sem=send_sem,
            recv_sem=recv_sem.at[last],
            device_id=(ctx, to),
            device_id_type=MESH,
        )

    def await_bytes(ref, sem):
        pltpu.make_async_copy(ref, ref, sem).wait()

    def others(first, count):
        return block.at[pl.ds(first, count), pl.ds(HALO, length - rows), :]

    half = n_y // 2
    ways = [(half, 1), (half, 0)]
    for dy in range(half - 1, 0, -1):
        ways += [(-dy, 1), (dy, 1), (-dy, 0), (dy, 0)]
    ways += [(0, 1)]

    def to_way(dy, swap):
        return 2 * lax.rem(y + dy + n_y, n_y) + (1 - core if swap else core)

    def send_queries():
        for way in ways:
            send_branch(0, 1, to_way(*way), q_send, q_recv).start()

    for way in ways:
        send_branch(1, 2, to_way(*way), kv_send, kv_recv).start()

    load_q.wait()

    @pl.when(last == 1)
    def _():
        send_queries()


    for i in range(MINOR - 1):

        @pl.when(i < x)
        def _(i=i):
            signal(x_ready, (z * MINOR + i, tp))

    for i in range(n_z - 2):

        @pl.when(i < z - 1)
        def _(i=i):
            signal(z_ready, (i * MINOR + x, tp))

    @pl.when(z > 0)
    def _():
        for i in range(MINOR):
            signal(up_ready, ((z - 1) * MINOR + i, tp))

    @pl.when(ctx > 0)
    def _():
        signal(edge_ready, (prv, tp))

    load_rates.wait()
    load_residues.wait()
    rate = rates[...]
    coef = residues[...] * jnp.sqrt(1.0 - jnp.exp(-2.0 * rate))
    pick_pole = (iota((groups, poles), 1) // order == iota((groups, poles), 0)).astype(F32)
    same_row = iota((order, poles), 1) % order == iota((order, poles), 0)
    rate_row = jnp.sum(jnp.where(same_row, over_groups(rate, pick_pole), 0.0), axis=0, keepdims=True)
    coef_row = jnp.sum(jnp.where(same_row, over_groups(coef, pick_pole), 0.0), axis=0, keepdims=True)
    pick_group = (iota((poles, groups), 0) // order == iota((poles, groups), 1)).astype(F32)
    same_col = iota((poles, order), 0) % order == iota((poles, order), 1)
    rate_col = jnp.sum(
        jnp.where(same_col, jnp.dot(pick_group, rate, precision=HIGHEST, preferred_element_type=F32), 0.0),
        axis=1,
        keepdims=True,
    )
    pick_channel = (iota((groups, channels), 1) // GROUP_CH == iota((groups, channels), 0)).astype(F32)
    rate_ch = over_groups(rate, pick_channel)
    decay_sub = jnp.exp(-rate_ch * SUB)
    decay = jnp.exp(-rate_ch * length)
    matching = iota((poles, channels), 0) // order == iota((poles, channels), 1) // GROUP_CH

    place = iota((SUB, poles), 0).astype(F32)
    falling = split(coef_row * jnp.exp(-rate_row * place))
    place = iota((poles, SUB), 1).astype(F32)
    rising = split(jnp.exp(rate_col * place))
    outof = split(jnp.exp(-rate_col * (SUB - 1.0 - place)))
    for b in range(subs):
        rows_b = pl.ds(b * SUB, SUB)
        place = (iota((SUB, poles), 0) + (b * SUB + 1)).astype(F32)
        high, low = split(coef_row * jnp.exp(-rate_row * place))
        inward[0, rows_b, :] = high
        inward[1, rows_b, :] = low
    causal = iota((SUB, SUB), 0) >= iota((SUB, SUB), 1)
    pole_group = iota((poles, SUB), 0) // order
    zero = jnp.zeros((), BF16)
    for g in range(groups):
        mine = pole_group == g
        part_g = (jnp.where(mine, rising[0], zero), jnp.where(mine, rising[1], zero))
        toeplitz[:, g * SUB : (g + 1) * SUB] = jnp.where(causal, dot3(falling, part_g), 0.0).astype(BF16)

    def send_edge(first, count, i):
        return pltpu.make_async_remote_copy(
            src_ref=block.at[pl.ds(first, count), pl.ds(length, HALO), :],
            dst_ref=block.at[pl.ds(first, count), pl.ds(0, HALO), :],
            send_sem=edge_send.at[i],
            recv_sem=edge_recv.at[i],
            device_id=(nxt, tp),
            device_id_type=MESH,
        )

    await_bytes(block.at[pl.ds(1, 2), block_rows(n_tp - 1), :], kv_recv.at[1])
    kv_edge = send_edge(1, 2, 0)

    @pl.when(ctx < n_ctx - 1)
    def _():
        pl.semaphore_wait(edge_ready, 1)
        kv_edge.start()

    await_bytes(others(1, 2), kv_send)

    @pl.when(last == 0)
    def _():
        send_queries()


    send_w = pltpu.make_async_remote_copy(
        src_ref=weight,
        dst_ref=w_sib,
        send_sem=pair_send.at[0],
        recv_sem=pair_recv.at[0],
        device_id=other,
        device_id_type=MESH,
    )
    send_w.start()


    await_bytes(others(1, 2), kv_recv.at[0])

    @pl.when(ctx > 0)
    def _():
        kv_edge.wait_recv()

    def widen(branch, slot):
        wide[slot, 0:HALO, :] = block[branch, 0:HALO, :].astype(F32)
        for start in range(0, length, SUB):
            wide[slot, HALO + start : HALO + start + SUB, :] = block[
                branch, HALO + start : HALO + start + SUB, :
            ].astype(F32)

    def short_conv(branch, rows_in, start):
        total = taps[branch, 0:1, :] * rows_in[HALO + start : HALO + start + ROWS_STEP, :]
        for j in range(1, TAPS):
            total = total + taps[branch, j : j + 1, :] * rows_in[HALO + start - j : HALO + start - j + ROWS_STEP, :]
        return total

    load_taps.wait()
    widen(1, 0)
    widen(2, 1)
    state = jnp.zeros((order, channels), F32)
    before = []
    for b in range(subs):
        for start in range(b * SUB, (b + 1) * SUB, ROWS_STEP):
            product[start : start + ROWS_STEP, :] = short_conv(1, wide.at[0], start) * short_conv(2, wide.at[1], start)
        spread = dot3(outof, split(product[b * SUB : (b + 1) * SUB, :]))
        spread = jnp.where(matching, spread, 0.0).reshape(groups, order, channels)
        before.append(state)
        state = decay_sub * state + jnp.sum(spread, axis=0)

    x_all[x] = state

    def send_x(step):
        return pltpu.make_async_remote_copy(
            src_ref=x_all.at[x],
            dst_ref=x_all.at[x],
            send_sem=x_send,
            recv_sem=x_recv,
            device_id=(x_at(step), tp),
            device_id_type=MESH,
        )

    @pl.when(x < MINOR - 1)
    def _():
        pl.semaphore_wait(x_ready, MINOR - 1 - x)

    for step in range(1, MINOR):
        send_x(step).start()

    def send_up(i):
        return pltpu.make_async_remote_copy(
            src_ref=x_all.at[x],
            dst_ref=up_all.at[x],
            send_sem=up_send,
            recv_sem=up_recv,
            device_id=((z + 1) * MINOR + i, tp),
            device_id_type=MESH,
        )

    @pl.when(z < n_z - 1)
    def _():
        pl.semaphore_wait(up_ready, MINOR)
        for i in range(MINOR):
            send_up(i).start()

    def expand(value):
        tiled = jnp.broadcast_to(value[None], (groups, order, channels)).reshape(poles, channels)
        return split(jnp.where(matching, tiled, 0.0))

    channel_group = iota((SUB, channels), 1) // GROUP_CH

    def local_sub(b):
        values = product[b * SUB : (b + 1) * SUB, :].astype(BF16)
        for g in range(groups):
            masked[g * SUB : (g + 1) * SUB, :] = jnp.where(channel_group == g, values, zero)
        total = dot(toeplitz[...], masked[...])
        if b > 0:
            total = total + dot3((inward[0, 0:SUB, :], inward[1, 0:SUB, :]), expand(before[b]))
        local[b * SUB : (b + 1) * SUB, :] = total

    local_sub(0)
    local_sub(1)

    q_edge = send_edge(0, 1, 1)
    await_bytes(block.at[pl.ds(0, 1), block_rows(n_tp - 1), :], q_recv.at[1])

    @pl.when(ctx < n_ctx - 1)
    def _():
        q_edge.start()

    await_bytes(x_all.at[pl.ds(0, MINOR - 1)], x_recv)
    row_total = x_all[0]
    row_before = jnp.zeros_like(row_total)
    for i in range(MINOR):
        if i > 0:
            row_total = decay * row_total + x_all[i]
        row_before = jnp.where(x > i, decay * row_before + x_all[i], row_before)

    z_all[z] = row_total

    def send_z(i):
        return pltpu.make_async_remote_copy(
            src_ref=z_all.at[z],
            dst_ref=z_all.at[z],
            send_sem=z_send.at[i],
            recv_sem=z_recv.at[z],
            device_id=(i * MINOR + x, tp),
            device_id_type=MESH,
        )

    @pl.when(z < n_z - 2)
    def _():
        pl.semaphore_wait(z_ready, n_z - 2 - z)

    for i in range(2, n_z):

        @pl.when(z < i - 1)
        def _(i=i):
            send_z(i).start()

    for b in range(2, subs):
        local_sub(b)

    await_bytes(others(0, 1), q_recv.at[0])

    @pl.when(ctx > 0)
    def _():
        q_edge.wait_recv()

    widen(0, 0)

    for i in range(n_z - 2):

        @pl.when(i < z - 1)
        def _(i=i):
            await_bytes(z_all.at[i], z_recv.at[i])

    @pl.when(z > 0)
    def _():
        await_bytes(up_all, up_recv)

    decay_row = jnp.exp(-rate_ch * (length * MINOR))
    above = jnp.zeros((order, channels), F32)
    for i in range(n_z - 2):
        above = jnp.where(z - 1 > i, decay_row * above + z_all[i], above)
    up_total = up_all[0]
    for i in range(1, MINOR):
        up_total = decay * up_total + up_all[i]
    above = jnp.where(z > 0, decay_row * above + up_total, above)
    incoming = row_before + jnp.exp(-rate_ch * (length * x).astype(F32)) * above

    per = SUB // (2 * rows)
    sign = 1 - 2 * core
    odd = 2 * lax.rem(y, 2) - 1
    first_sub = lax.div(lax.rem(y + n_y // 2, n_y), 2)
    order_subs = [lax.rem(first_sub + subs + odd * i, subs) for i in (0, 1, -1, 2)]

    def send_gated(b, i):
        return pltpu.make_async_remote_copy(
            src_ref=gated.at[pl.ds(b * per, per), 1 - core],
            dst_ref=sibling.at[pl.ds(b * per, per)],
            send_sem=pair_send.at[1],
            recv_sem=pair_recv.at[1 + i],
            device_id=other,
            device_id_type=MESH,
        )

    carried = expand(incoming)
    for i, b in enumerate(order_subs):
        rows_b = pl.ds(pl.multiple_of(b * SUB, SUB), SUB)
        total = local[rows_b, :] + dot3((inward[0, rows_b, :], inward[1, rows_b, :]), carried)
        rows_in = wide.at[0, pl.ds(pl.multiple_of(b * SUB, SUB), HALO + SUB), :]
        query = jnp.concatenate([short_conv(0, rows_in, start) for start in range(0, SUB, ROWS_STEP)], axis=0)
        value = (query * total).astype(BF16)
        gated[pl.ds(b * per, per)] = value.reshape(per, 2, rows, channels)
        send_gated(b, i // 2).start()

    def y_at(step):
        return lax.rem(y + sign * step + n_y, n_y)

    def ring(k, piece):
        ahead = y_at(1) if k < FAR else y_at(-1)
        cols = pl.ds(pl.multiple_of(piece * COLS, COLS), COLS)
        return pltpu.make_async_remote_copy(
            src_ref=going.at[k, :, cols],
            dst_ref=coming.at[k, :, cols],
            send_sem=ring_send,
            recv_sem=ring_recv.at[k, piece],
            device_id=(ctx, 2 * ahead + core),
            device_id_type=MESH,
        )

    def target(k):
        return y_at(FAR - k) if k < FAR else y_at(-(NEAR - (k - FAR)))

    def gather(chips):
        own = jnp.concatenate([gated[chip, core] for chip in chips], axis=0)
        return own, jnp.concatenate([sibling[chip] for chip in chips], axis=0)

    def project(pair, cols):
        return dot(pair[0], w_own[:, cols]) + dot(pair[1], w_sib[:, cols])

    half_bytes = sibling.at[pl.ds(0, n_y // 2)]
    load_w.wait()
    send_w.wait()
    await_bytes(half_bytes, pair_recv.at[1])
    leading = gather([target(0), target(FAR)])

    @pl.loop(0, pieces)
    def _(piece):
        cols = pl.ds(pl.multiple_of(piece * COLS, COLS), COLS)
        total = project(leading, cols).astype(BF16)
        for i, k in enumerate((0, FAR)):
            going[k, :, cols] = total[i * rows : (i + 1) * rows]
            ring(k, piece).start()

    later = [k for hop in range(1, FAR) for k in (hop, FAR + hop) if k < FAR + NEAR]
    await_bytes(half_bytes, pair_recv.at[2])
    following = gather([target(k) for k in later] + [y])

    @pl.loop(0, pieces)
    def _(piece):
        cols = pl.ds(pl.multiple_of(piece * COLS, COLS), COLS)
        part[:, :, cols] = project(following, cols).reshape(len(later) + 1, rows, COLS)

    for hop in range(1, FAR):

        @pl.loop(0, pieces)
        def _(piece, hop=hop):
            cols = pl.ds(pl.multiple_of(piece * COLS, COLS), COLS)
            for k in (hop, FAR + hop):
                if k < FAR + NEAR:
                    ring(k - 1, piece).wait_recv()
                    going[k, :, cols] = (
                        part[later.index(k), :, cols] + coming[k - 1, :, cols].astype(F32)
                    ).astype(BF16)
                    ring(k, piece).start()

    load_r.wait()

    @pl.loop(0, pieces)
    def _(piece):
        cols = pl.ds(pl.multiple_of(piece * COLS, COLS), COLS)
        ring(FAR - 1, piece).wait_recv()
        ring(FAR + NEAR - 1, piece).wait_recv()
        total = part[len(later), :, cols] + coming[FAR - 1, :, cols].astype(F32)
        total = total + coming[FAR + NEAR - 1, :, cols].astype(F32)
        out[:, cols] = (res_in[:, cols].astype(F32) + total).astype(BF16)

    @pl.when(ctx < n_ctx - 1)
    def _():
        kv_edge.wait_send()
        q_edge.wait_send()

    await_bytes(others(0, 1), q_send)
    await_bytes(x_all.at[pl.ds(0, MINOR - 1)], x_send)
    for i in range(2, n_z):

        @pl.when(z < i - 1)
        def _(i=i):
            send_z(i).wait_send()

    @pl.when(z < n_z - 1)
    def _():
        await_bytes(up_all, up_send)

    await_bytes(sibling, pair_send.at[1])
    await_bytes(going, ring_send)


def body(n_ctx, n_tp, features, residual, short_weight, rates, residues, out_weight):
    feat = jnp.transpose(features, (1, 0, 2))
    taps = jnp.transpose(short_weight, (1, 0, 2))
    rows, width = residual.shape
    channels = taps.shape[2]
    groups, order = rates.shape
    poles = groups * order
    length = n_tp * rows
    n_y = n_tp // 2
    pieces = width // COLS
    slots = FAR + NEAR
    n_z = n_ctx // MINOR
    hbm = pltpu.MemorySpace.HBM
    any_spec = pl.BlockSpec(memory_space=hbm)
    args = (feat, residual, taps, rates, residues, out_weight)
    vmem_spec = pl.BlockSpec(memory_space=pltpu.VMEM)
    dma = pltpu.SemaphoreType.DMA
    regular = pltpu.SemaphoreType.REGULAR
    return pl.pallas_call(
        functools.partial(kernel, n_ctx, n_tp),
        out_shape=jax.ShapeDtypeStruct((rows, width), BF16),
        in_specs=[any_spec] * 6,
        out_specs=vmem_spec,
        scratch_shapes=[
            pltpu.VMEM((3, rows, width), BF16),
            pltpu.VMEM((3, TAPS, channels), F32),
            pltpu.VMEM((groups, order), F32),
            pltpu.VMEM((groups, order), F32),
            pltpu.VMEM((3, HALO + length, channels), BF16),
            pltpu.VMEM((2, HALO + length, channels), F32),
            pltpu.VMEM((length, channels), F32),
            pltpu.VMEM((length, channels), F32),
            pltpu.VMEM((SUB, groups * SUB), BF16),
            pltpu.VMEM((groups * SUB, channels), BF16),
            pltpu.VMEM((2, length, poles), BF16),
            pltpu.VMEM((n_y, 2, rows, channels), BF16),
            pltpu.VMEM((n_y, rows, channels), BF16),
            pltpu.VMEM((channels, width), BF16),
            pltpu.VMEM((channels, width), BF16),
            pltpu.VMEM((slots - 1, rows, width), F32),
            pltpu.VMEM((slots, rows, width), BF16),
            pltpu.VMEM((slots, rows, width), BF16),
            pltpu.VMEM((rows, width), BF16),
            pltpu.VMEM((MINOR, order, channels), F32),
            pltpu.VMEM((n_z, order, channels), F32),
            pltpu.VMEM((MINOR, order, channels), F32),
            dma((7,)),
            regular,
            regular,
            regular,
            regular,
            dma,
            dma,
            dma,
            dma((2,)),
            dma,
            dma((2,)),
            dma((2,)),
            dma((2,)),
            dma,
            dma,
            dma((n_z,)),
            dma((n_z,)),
            dma((2,)),
            dma((3,)),
            dma,
            dma((slots, pieces)),
        ],
        compiler_params=pltpu.CompilerParams(
            collective_id=0, has_side_effects=True, vmem_limit_bytes=48 * 1024 * 1024
        ),
    )(*[pltpu.with_memory_space_constraint(arg, hbm) for arg in args])


def solution(mesh):
    in_specs = (
        P(("ctx", "tp"), None, None),
        P(("ctx", "tp"), None),
        P(None, None, "tp"),
        P("tp", None),
        P("tp", None),
        P("tp", None),
    )
    out_specs = P(("ctx", "tp"), None)
    run = functools.partial(body, mesh.shape["ctx"], mesh.shape["tp"])
    return jax.shard_map(run, mesh=mesh, in_specs=in_specs, out_specs=out_specs, check_vma=False)
```
